32 devices in a mesh: groups: 2 (over x), ctx: 16 (over z, y, core).
Axes of the slice: x: 2, y: 2, z: 4, core: 2. Of those that a mesh axis runs over, the one named last changes fastest.
Arguments:
- queries: bfloat16 [2560, 4096], P(('groups', 'ctx')), parts along dimension 0, may hold values from -200 to 200
- fresh_key_value: bfloat16 [2, 2560, 512], P(None, ('groups', 'ctx')), parts along dimension 1, may hold values from -6 to 6
- cache_key_value: bfloat16 [2, 4096, 512], P(None, ('groups', 'ctx')), parts along dimension 1, may hold values from -6 to 6
- residual: bfloat16 [2560, 2048], P(('groups', 'ctx')), parts along dimension 0, may hold values from -6 to 6
- norm_gain: float32 [2048], replicated, may hold values from 0.5 to 2
- out_proj: bfloat16 [4096, 2048], P('ctx'), may hold values from -0.09375 to 0.09375
- w_gate_up: bfloat16 [32, 2048, 1536], P('ctx'), may hold values from -0.125 to 0.125
- w_down: bfloat16 [32, 768, 2048], P('ctx'), may hold values from -0.21875 to 0.21875
- route_ids: int32 [2560, 8], P(('groups', 'ctx')), parts along dimension 0, may hold values from 0 to 31, all different within a row; in each aligned block of 80 rows (0 to 79, 80 to 159, ...) at most 30 rows name the same one
- route_weights: float32 [2560, 8], P(('groups', 'ctx')), parts along dimension 0, may hold values from 0.05 to 1
- placement: int32 [32], replicated, may hold values from 0 to 31, each once
Outputs:
- hidden: bfloat16 [2560, 2048], P(('groups', 'ctx')), parts along dimension 0
- expert_out: bfloat16 [2560, 2048], P(('groups', 'ctx')), parts along dimension 0
The draws below stay inside these ranges and needn't reach their ends.
There are 2 independent parts, one for each index of `groups`. The reference program is written for one: setup_inputs(seed, part) draws one part's arguments, and reference() takes and returns one part's arrays. A program takes and returns all parts, laid end to end along the dimension named above; an argument that names none is the same for every part. Nothing has to cross between parts.
Inputs may be any that keep to these rules, and one draw needn't show every extreme that they name: `route_ids`: among the rows of one index of ctx, no expert is named by more than 30 rows, a bound that some block reaches. `placement`: every slot once; slot s is the first index of w_gate_up and w_down.
All inputs are finite; a program needn't handle non-finite values.
Results may differ from the reference program's by a relative error of at most 0.017.
Values may be sent and summed in bfloat16 or wider, within the bound.
A program may use at most 128 MiB of HBM per device.

```python
import math
import jax
import jax.numpy as jnp
import numpy as np
from jax import lax

D = 2048
QUERY_HEADS = 32
KEY_VALUE_HEADS = 4
HEAD_SIZE = 128
FF = 768
TOPK = 8
ROWS_DEV = 80
EXPERTS = 32
WINDOW_ROWS = 1280
CACHED_KEYS = 2048
MOST = 30
N_CTX = 16


def attention_pair(key):
    query_key = jax.random.fold_in(key, 101)
    stored_key = jax.random.fold_in(key, 102)
    random_value_key = jax.random.fold_in(key, 103)
    queries = 2.5 * jax.random.truncated_normal(query_key, -6.0, 6.0, (WINDOW_ROWS, QUERY_HEADS * HEAD_SIZE), jnp.float32)
    stored_keys = jax.random.truncated_normal(stored_key, -6.0, 6.0, (CACHED_KEYS, KEY_VALUE_HEADS * HEAD_SIZE), jnp.float32)
    stored_values = jax.random.truncated_normal(random_value_key, -6.0, 6.0, (CACHED_KEYS, KEY_VALUE_HEADS * HEAD_SIZE), jnp.float32)
    return (queries, stored_keys, stored_values)


def draw_queries(key, part):
    queries, stored_keys, stored_values = attention_pair(key)
    return queries.astype(jnp.bfloat16)


def draw_cache_key_value(key, part):
    queries, stored_keys, stored_values = attention_pair(key)
    return jnp.stack([stored_keys, stored_values], axis=0).astype(jnp.bfloat16)


def level_of(rng, dims, cuts, low, high):
    level = 1.0
    for dim, blocks in cuts:
        steps = jax.random.uniform(jax.random.fold_in(jax.random.fold_in(rng, 6), dim), (blocks,), jnp.float32, low / len(cuts), high / len(cuts))
        level = level * jnp.repeat(jnp.exp(steps), dims[dim] // blocks).reshape((-1,) + (1,) * (len(dims) - 1 - dim))
    return level


def routed_block(own_key, own, number, rows, number_of, top, reach, slope):
    ranking = jax.random.permutation(own_key, number_of)
    heavy_load, common = shares(number_of, rows * top, reach, slope, True), shares(number_of, rows * top, reach, slope, False)
    places = jnp.arange(number_of)

    def named(sizes, turn):
        used = int((sizes > 0).sum())
        fixed = max(1, used // 4)
        shifted = fixed + (places - fixed + turn * (used - fixed)) % max(1, number_of - fixed)
        return jnp.zeros((number_of,), jnp.int32).at[ranking[jnp.where(places < fixed, places, shifted)]].set(jnp.asarray(sizes, jnp.int32))

    sizes = jnp.where(number % 4 == 0, named(heavy_load, number // 4), named(common, number - number // 4 - 1))
    mixed = jax.random.permutation(jax.random.fold_in(own, 3), number_of)
    giver, taker = mixed[0:number_of // 2 * 2:2], mixed[1:number_of // 2 * 2:2]
    margin = jnp.minimum(sizes[giver] - 1, reach - sizes[taker]) // 2
    margin = jnp.where((giver == ranking[0]) | (taker == ranking[0]) | (sizes[taker] == 0), 0, jnp.maximum(margin, 0))
    shifted = jax.random.randint(jax.random.fold_in(own, 4), (number_of // 2,), 0, 1 << 20) % (margin + 1)
    sizes = sizes.at[giver].add(-shifted).at[taker].add(shifted)
    labels = jnp.searchsorted(jnp.cumsum(sizes), jnp.arange(rows * top), side="right").astype(jnp.int32)
    listing = labels.reshape(top, rows).T
    listing = listing[jax.random.permutation(jax.random.fold_in(own, 1), rows)]
    turn = jax.random.randint(jax.random.fold_in(own, 2), (rows, 1), 0, top)
    return jnp.take_along_axis(listing, (jnp.arange(top)[None, :] + turn) % top, axis=1)


def shares(number_of, total, bound, lean, full):
    weights = [(1 << 20) // math.isqrt(rank ** lean) + 1 for rank in range(1, number_of + 1)]
    largest = bound if full else min(bound, max(-(-total // number_of), total * weights[0] // sum(weights)))
    least = 1 if total - largest >= number_of - 1 else 0
    holding, surplus = [largest] + [least] * (number_of - 1), total - largest - least * (number_of - 1)
    while surplus > 0:
        candidates = [i for i in range(1, number_of) if holding[i] < largest] or [i for i in range(1, number_of) if holding[i] < bound]
        whole, remaining = sum([weights[i] for i in candidates]), surplus
        for i in candidates:
            addition = min(bound - holding[i], max(1, remaining * weights[i] // whole), surplus)
            holding[i] = holding[i] + addition
            surplus = surplus - addition
    return np.array(holding)


def centred(own_key, extent, spread, most, cuts=(), kind=jnp.bfloat16):
    values = jax.random.normal(own_key, extent, jnp.float32) * spread
    if len(cuts) > 0:
        values = level_of(own_key, extent, cuts, -0.22, 0.18) * values
    return jnp.clip(values, min=-most, max=most).astype(kind)


def setup_inputs(seed: int = 0, part: int = 0) -> dict:
    key_list = jax.random.split(jax.random.key(seed), 12)
    part_keys = jax.random.split(jax.random.fold_in(key_list[11], part), 12)
    queries = draw_queries(jax.random.fold_in(jax.random.fold_in(key_list[11], part), 71), part)
    fresh_key_value = centred(part_keys[1], (2, WINDOW_ROWS, KEY_VALUE_HEADS * HEAD_SIZE), 1.0, 6.0, ((1, 16),))
    cache_key_value = draw_cache_key_value(jax.random.fold_in(jax.random.fold_in(key_list[11], part), 71), part)
    residual = centred(part_keys[3], (WINDOW_ROWS, D), 1.0, 6.0, ((0, 16),))
    norm_gain = jnp.clip(jnp.exp(jax.random.uniform(key_list[4], (D,), jnp.float32, math.log(0.5), math.log(2.0))), 0.5, 2.0)
    out_proj = centred(key_list[5], (QUERY_HEADS * HEAD_SIZE, D), (QUERY_HEADS * HEAD_SIZE) ** -0.5, 0.09375, ((0, 16),))
    w_gate_up = centred(key_list[6], (EXPERTS, D, 2 * FF), D ** -0.5, 0.125, ((0, 16),))
    w_down = centred(key_list[7], (EXPERTS, FF, D), FF ** -0.5, 0.21875, ((0, 16),))
    route_ids_keys = jax.random.split(jax.random.fold_in(part_keys[8], 1), WINDOW_ROWS // ROWS_DEV)
    route_ids_turns = jax.random.permutation(jax.random.fold_in(part_keys[8], 3), WINDOW_ROWS // ROWS_DEV)
    route_ids = jax.vmap(lambda own, number: routed_block(jax.random.fold_in(part_keys[8], 2), own, number, ROWS_DEV, EXPERTS, TOPK, MOST, 2))(route_ids_keys, route_ids_turns).reshape((WINDOW_ROWS, TOPK))
    route_weights = jnp.clip(jnp.exp(math.log(1.0) - 2.9957323 * jax.random.uniform(part_keys[9], (WINDOW_ROWS, TOPK), jnp.float32) ** level_of(part_keys[9], (WINDOW_ROWS, TOPK), ((0, 16),), -0.2, 0.2)), 0.05, 1.0)
    placement = jax.random.permutation(key_list[10], EXPERTS).astype(jnp.int32)
    return dict(queries=queries, fresh_key_value=fresh_key_value, cache_key_value=cache_key_value, residual=residual, norm_gain=norm_gain, out_proj=out_proj, w_gate_up=w_gate_up, w_down=w_down, route_ids=route_ids, route_weights=route_weights, placement=placement)


def reference(queries, fresh_key_value, cache_key_value, residual, norm_gain, out_proj, w_gate_up, w_down, route_ids, route_weights, placement):
    count_of_rows = queries.shape[0]
    query_group_width = QUERY_HEADS // KEY_VALUE_HEADS
    scale_for_scores = HEAD_SIZE ** (-0.5)
    stored_keys = cache_key_value[0].astype(jnp.float32).reshape(-1, KEY_VALUE_HEADS, HEAD_SIZE)
    stored_values = cache_key_value[1].astype(jnp.float32).reshape(-1, KEY_VALUE_HEADS, HEAD_SIZE)
    block_of_rows = math.gcd(count_of_rows, 128)

    def attend(pieces):
        block_of_queries, self_key, self_value = pieces
        widened_query = block_of_queries.astype(jnp.float32).reshape(block_of_rows, KEY_VALUE_HEADS, query_group_width, HEAD_SIZE)
        scores = jnp.einsum('rkgd,jkd->rkgj', widened_query, stored_keys) * scale_for_scores
        self_score = jnp.einsum('ejaz,ejz->eja', widened_query, self_key.astype(jnp.float32).reshape(block_of_rows, KEY_VALUE_HEADS, HEAD_SIZE)) * scale_for_scores
        peak_value = jnp.maximum(lax.optimization_barrier(jnp.max(scores, axis=-1)), self_score)
        weights = jnp.exp(scores - peak_value[..., None])
        self_weight = jnp.exp(self_score - peak_value)
        totals = lax.optimization_barrier(jnp.sum(weights, axis=-1)) + self_weight
        weighted_total = jnp.einsum('rkgj,jkd->rkgd', weights.astype(jnp.bfloat16).astype(jnp.float32), stored_values)
        weighted_total = weighted_total + self_weight[..., None] * self_value.astype(jnp.float32).reshape(block_of_rows, KEY_VALUE_HEADS, 1, HEAD_SIZE)
        return (weighted_total / totals[..., None]).reshape(block_of_rows, QUERY_HEADS * HEAD_SIZE).astype(jnp.bfloat16)

    def blocked(array):
        return array.reshape(count_of_rows // block_of_rows, block_of_rows, array.shape[-1])
    attention = lax.map(attend, (blocked(queries), blocked(fresh_key_value[0]), blocked(fresh_key_value[1]))).reshape(count_of_rows, QUERY_HEADS * HEAD_SIZE)
    projected = jnp.dot(attention, out_proj, preferred_element_type=jnp.float32)
    hidden = (residual.astype(jnp.float32) + projected).astype(jnp.bfloat16)
    hidden_wide = hidden.astype(jnp.float32)
    normed = (hidden_wide * lax.rsqrt(lax.optimization_barrier(jnp.mean(hidden_wide * hidden_wide, axis=-1, keepdims=True)) + 1e-06) * norm_gain).astype(jnp.bfloat16)
    expert_count = placement.shape[0]
    slot_ids = placement[route_ids].reshape(-1).astype(jnp.int32)
    assigned = slot_ids.shape[0]
    sorted_idx = jnp.argsort(slot_ids, stable=True).astype(jnp.int32)
    expert_range = jnp.arange(expert_count, dtype=jnp.int32)
    counts = lax.optimization_barrier(jnp.sum((slot_ids[:, None] == expert_range[None, :]).astype(jnp.int32), axis=0)).astype(jnp.int32)
    starts = (jnp.cumsum(counts) - counts).astype(jnp.int32)
    capacity = N_CTX * MOST
    offsets = jnp.arange(capacity, dtype=jnp.int32)
    picked = jnp.minimum(starts[:, None] + offsets[None, :], assigned - 1).astype(jnp.int32)
    filled = offsets[None, :] < counts[:, None]
    source_rows = (sorted_idx[picked] // TOPK).astype(jnp.int32)

    def expert_run(pieces):
        slot_index, row_index, keep_rows = pieces
        inputs = jnp.where(keep_rows[:, None], normed[row_index], jnp.zeros((), jnp.bfloat16))
        both = jnp.dot(inputs, w_gate_up[slot_index], preferred_element_type=jnp.float32)
        active = (jax.nn.silu(both[:, :FF]) * both[:, FF:]).astype(jnp.bfloat16)
        return jnp.dot(active, w_down[slot_index], preferred_element_type=jnp.float32).astype(jnp.bfloat16)
    results = lax.map(expert_run, (expert_range, source_rows, filled))
    ranks = jnp.zeros((assigned,), jnp.int32).at[sorted_idx].set(jnp.arange(assigned, dtype=jnp.int32) - starts[slot_ids[sorted_idx]])
    routed = results[slot_ids, ranks].reshape(count_of_rows, TOPK, D).astype(jnp.float32)
    gate_share = route_weights / lax.optimization_barrier(jnp.sum(route_weights, axis=-1, keepdims=True))
    expert_out = lax.optimization_barrier(jnp.sum(gate_share[..., None] * routed, axis=1)).astype(jnp.bfloat16)
    return (hidden, expert_out)
```

```python
import functools
import types
from collections import deque

import jax
import jax.numpy as jnp
from jax import lax
from jax.experimental import pallas as pl
from jax.experimental.pallas import tpu as pltpu
from jax.sharding import PartitionSpec as P

QUERY_HEADS = 32
KEY_VALUE_HEADS = 4
HEAD_SIZE = 128
TOPK = 8
COLUMNS_STEP = 512
FF_STEP = 256
LANES = 128

epsilon = 1e-06

VMEM = pl.BlockSpec(memory_space=pltpu.VMEM)
ANY = pl.BlockSpec(memory_space=pl.ANY)
RIGHT, LEFT = 0, 1
PAIRS = ((RIGHT, 0), (LEFT, 1), (RIGHT, 1), (LEFT, 0))


def chip_at(q, m):
    return jnp.where(q < m // 2, 2 * q, 2 * (m - 1 - q) + 1)


def place_of(chip, m):
    return jnp.where(chip % 2 == 0, chip // 2, m - 1 - chip // 2)


def flip(value, key, size):
    total, bit = 0, 1
    while bit < size:
        total = total + (value // bit + key // bit) % 2 * bit
        bit *= 2
    return total


def greet(others):
    barrier = pltpu.get_barrier_semaphore()
    for other in others:
        pl.semaphore_signal(
            barrier, inc=1, device_id={"ctx": other}, device_id_type=pl.DeviceIdType.MESH
        )
    pl.semaphore_wait(barrier, len(others))


def remote(src, dst, send, recv, other):
    return pltpu.make_async_remote_copy(
        src_ref=src,
        dst_ref=dst,
        send_sem=send,
        recv_sem=recv,
        device_id={"ctx": other},
        device_id_type=pl.DeviceIdType.MESH,
    )


def landed(piece, sem):
    pltpu.make_async_copy(piece, piece, sem).wait()


def travels(way, half, d, reach):
    return d < reach or (d == reach and half == way)


def block_places(rows, experts):
    most = max(2, 3 * rows * TOPK // (2 * experts))
    return -(-most // 16) * 16


def whole_kernel(
    n,
    names,
    queries,
    fresh,
    cache,
    proj,
    gate_up,
    down,
    residual,
    gain,
    ids,
    route,
    placement,
    hidden,
    result,
    *scratch,
):
    s = types.SimpleNamespace(**dict(zip(names, scratch)))
    m, planes, reach = n // 2, n // 4, n // 4
    rows, width = residual.shape
    half_width = width // 2
    cols = [pl.ds(h * half_width, half_width) for h in range(2)]
    local_count, _, wide = gate_up.shape
    ff = wide // 2
    experts = placement.shape[1]
    places = s.rows_in.shape[2]
    per = QUERY_HEADS // n
    head_width = per * HEAD_SIZE
    share = n // KEY_VALUE_HEADS

    me = lax.axis_index("ctx")
    core, chip = me % 2, me // 2
    y, z = chip % 2, chip // 2

    def device(zz, yy, cc):
        return (zz * 2 + yy) * 2 + cc

    mate = device(z, y, 1 - core)
    across = device(z, 1 - y, core)
    started = []

    def send(src, dst, send_sem, recv_sem, other):
        copy = remote(src, dst, send_sem, recv_sem, other)
        copy.start()
        started.append(copy)

    def finish_sends():
        while started:
            started.pop(0).wait_send()

    greet([(me + j) % n for j in range(1, n)])

    mine, rank = me // share, me % share
    sources = ((cache, s.kv), (fresh, s.own))

    def lanes_of(head):
        return pl.ds(pl.multiple_of(head * HEAD_SIZE, HEAD_SIZE), HEAD_SIZE)

    local = []
    for kind, (src, dst) in enumerate(sources):
        copy = pltpu.make_async_copy(
            src.at[:, :, lanes_of(mine)], dst.at[:, mine, rank], s.kv_recv.at[kind, 0]
        )
        copy.start()
        local.append(copy)

    def spread_kv(kind):
        src, dst = sources[kind]
        for i in range(1, KEY_VALUE_HEADS):
            head = (mine + i) % KEY_VALUE_HEADS
            send(
                src.at[:, :, lanes_of(head)],
                dst.at[:, mine, rank],
                s.kv_send.at[kind, i],
                s.kv_recv.at[kind, i],
                head * share + rank,
            )

    spread_kv(0)
    spread_kv(1)

    copy = pltpu.make_async_copy(
        queries.at[:, pl.ds(pl.multiple_of(me * head_width, LANES), head_width)],
        s.q.at[me],
        s.q_recv.at[me],
    )
    copy.start()
    number = 0
    for key in range(planes - 1, -1, -1):
        for dy in (1, 0):
            for dc in (0, 1):
                if (key, dy, dc) == (0, 0, 0):
                    continue
                other = device(flip(z, key, planes), (y + dy) % 2, (core + dc) % 2)
                send(
                    queries.at[:, pl.ds(pl.multiple_of(other * head_width, LANES), head_width)],
                    s.q.at[me],
                    s.q_send.at[number],
                    s.q_recv.at[me],
                    other,
                )
                number += 1

    send(proj, s.proj_mate, s.mate_send.at[m], s.mate_recv.at[m], mate)
    weights = [
        pltpu.make_async_copy(proj, s.proj_mine, s.load.at[0]),
        pltpu.make_async_copy(gate_up, s.gate_up, s.load.at[1]),
        pltpu.make_async_copy(down, s.down, s.load.at[2]),
    ]
    for copy in weights:
        copy.start()

    scores = route[...]
    scores = scores / jnp.sum(scores, axis=-1, keepdims=True)
    listed = lax.broadcasted_iota(jnp.int32, (rows, experts), 1)
    by_expert = jnp.zeros((rows, experts), jnp.float32)
    for k in range(TOPK):
        by_expert = by_expert + jnp.where(listed == ids[:, k : k + 1], scores[:, k : k + 1], 0.0)
    by_expert = jnp.concatenate(
        [by_expert, jnp.zeros((LANES - rows, experts), jnp.float32)], axis=0
    ).astype(jnp.bfloat16)
    moved = jnp.where(
        lax.broadcasted_iota(jnp.int32, (experts, experts), 0) == placement[...], 1.0, 0.0
    ).astype(jnp.bfloat16)
    by_slot = lax.dot_general(
        moved, by_expert, (((1,), (1,)), ((), ())), preferred_element_type=jnp.float32
    )
    named = jnp.where(by_slot > 0, 1.0, 0.0)
    before = jnp.where(
        lax.broadcasted_iota(jnp.int32, (LANES, LANES), 0)
        < lax.broadcasted_iota(jnp.int32, (LANES, LANES), 1),
        1.0,
        0.0,
    ).astype(jnp.bfloat16)
    ranks = jnp.dot(named.astype(jnp.bfloat16), before, preferred_element_type=jnp.float32)
    ranks = jnp.where(by_slot > 0, ranks, -1.0)
    pair = 2 * local_count
    for c in range(m):
        s.table[c, 0:pair, :] = ranks[c * pair : (c + 1) * pair]
        s.table[c, pair : 2 * pair, :] = by_slot[c * pair : (c + 1) * pair]
    s.tables[me] = s.table[chip]
    for j in range(1, n):
        other = (me + j) % n
        send(
            s.table.at[other // 2], s.tables.at[me], s.t_send.at[j], s.t_recv.at[j], other
        )

    steps = []
    bit = 2
    while bit < share:
        steps.append(bit)
        bit *= 2

    for kind in range(2):
        dst = sources[kind][1]

        def slot(g, r, dst=dst):
            return dst.at[:, g, r]

        local[kind].wait()
        order = [(mine + KEY_VALUE_HEADS - i) % KEY_VALUE_HEADS for i in range(KEY_VALUE_HEADS)]
        held = [0]
        for number, bit in enumerate(steps):
            for i, g in enumerate(order):
                if number == 0 and i > 0:
                    landed(slot(g, rank), s.kv_recv.at[kind, i])
                for k in held:
                    send(
                        slot(g, flip(rank, k, share)),
                        slot(g, flip(rank, k, share)),
                        s.fw_send.at[kind, i, number, k // 2],
                        s.fw_recv.at[kind, i, k + bit],
                        mine * share + flip(rank, bit, share),
                    )
            for i, g in enumerate(order):
                for k in held:
                    landed(slot(g, flip(rank, k + bit, share)), s.fw_recv.at[kind, i, k + bit])
                    if number == len(steps) - 1:
                        send(
                            slot(g, flip(rank, k + bit, share)),
                            slot(g, flip(rank, k + bit, share)),
                            s.fw_send.at[kind, i, len(steps), (k + bit) // 2],
                            s.fw_recv.at[kind, i, k + bit + 1],
                            mate,
                        )
                    if number == len(steps) - 1:
                        send(
                            slot(g, flip(rank, k, share)),
                            slot(g, flip(rank, k, share)),
                            s.fw_send.at[kind, i, len(steps), k // 2],
                            s.fw_recv.at[kind, i, k + 1],
                            mate,
                        )
            held = held + [k + bit for k in held]
    for kind in range(2):
        dst = sources[kind][1]
        for i in range(KEY_VALUE_HEADS):
            g = (mine + KEY_VALUE_HEADS - i) % KEY_VALUE_HEADS
            for k in range(0, share, 2):
                landed(dst.at[:, g, flip(rank, k + 1, share)], s.fw_recv.at[kind, i, k + 1])
    landed(s.proj_mate, s.mate_recv.at[m])
    weights[0].wait()

    key_count = s.kv.shape[3]
    scale = HEAD_SIZE ** (-0.5)

    def target(t):
        return flip(z, planes - 1 - t, planes)

    def attend(t):
        @pl.loop(0, 2)
        def _(line):
            c = target(t) * 2 + (y + 1 + line) % 2
            for cc in range(2):
                landed(s.q.at[2 * c + cc], s.q_recv.at[2 * c + cc])
            keys = s.kv[0].reshape(n * key_count, HEAD_SIZE)
            values = s.kv[1].reshape(n * key_count, HEAD_SIZE)
            fresh_key = s.own[0, (2 * c) // share, pl.ds((2 * c) % share, 2)]
            fresh_key = fresh_key.reshape(2 * rows, HEAD_SIZE).astype(jnp.float32)
            fresh_value = s.own[1, (2 * c) // share, pl.ds((2 * c) % share, 2)]
            fresh_value = fresh_value.reshape(2 * rows, HEAD_SIZE).astype(jnp.float32)
            for h in range(per):
                lanes = slice(h * HEAD_SIZE, (h + 1) * HEAD_SIZE)
                q = s.q[pl.ds(2 * c, 2), :, lanes].reshape(2 * rows, HEAD_SIZE)
                scores = lax.dot_general(
                    q, keys, (((1,), (1,)), ((), ())), preferred_element_type=jnp.float32
                )
                own = jnp.sum(q.astype(jnp.float32) * fresh_key, axis=-1, keepdims=True)
                peak = jnp.maximum(own, jnp.max(scores, axis=-1, keepdims=True))
                weight = jnp.exp((scores - peak) * scale)
                own = jnp.exp((own - peak) * scale)
                total = jnp.sum(weight, axis=-1, keepdims=True) + own
                mixed = jnp.dot(
                    weight.astype(jnp.bfloat16), values, preferred_element_type=jnp.float32
                )
                mixed = (mixed + own * fresh_value) / total
                s.att[c, :, :, lanes] = mixed.astype(jnp.bfloat16).reshape(2, rows, HEAD_SIZE)
            remote(
                s.att.at[c, 1 - core],
                s.att_mate.at[c],
                s.mate_send.at[c],
                s.mate_recv.at[c],
                mate,
            ).start()

    def project(t):
        zd = target(t)
        chips = [zd * 2 + (1 - y), zd * 2 + y]
        for c in chips:
            landed(s.att_mate.at[c], s.mate_recv.at[c])
        left = jnp.concatenate([s.att[c, core] for c in chips], axis=0)
        left_mate = jnp.concatenate([s.att_mate[c] for c in chips], axis=0)
        for half in range(2):

            @pl.loop(0, half_width // COLUMNS_STEP)
            def _(i):
                part = pl.ds(pl.multiple_of(i * COLUMNS_STEP, COLUMNS_STEP), COLUMNS_STEP)
                at = pl.ds(
                    pl.multiple_of(half * half_width + i * COLUMNS_STEP, COLUMNS_STEP), COLUMNS_STEP
                )
                product = jnp.dot(
                    left, s.proj_mine[:, at], preferred_element_type=jnp.float32
                ) + jnp.dot(left_mate, s.proj_mate[:, at], preferred_element_type=jnp.float32)
                s.outgoing[0, zd, half, :, part] = product[:rows].astype(jnp.bfloat16)
                s.part[t % 2, half, :, part] = product[rows:]

            remote(
                s.outgoing.at[0, zd, half],
                s.y_in.at[zd, half],
                s.y_send.at[zd, half],
                s.y_recv.at[zd, half],
                across,
            ).start()

    def from_line(zd, way, half):
        landed(s.incoming.at[way, zd, half], s.z_recv.at[way, zd, half])

    def relay(t):
        zd = target(t)
        way = jnp.where(zd > z, RIGHT, LEFT)
        inner = jnp.where(zd > z, z > 0, z < planes - 1)
        other = device(jnp.where(zd > z, z + 1, z - 1), y, core)
        for half in range(2):
            landed(s.y_in.at[zd, half], s.y_recv.at[zd, half])

            @pl.when(inner)
            def _():
                from_line(zd, way, half)
                total = (
                    s.part[t % 2, half]
                    + s.y_in[zd, half].astype(jnp.float32)
                    + s.incoming[way, zd, half].astype(jnp.float32)
                )
                s.outgoing[1, zd, half] = total.astype(jnp.bfloat16)

            @pl.when(jnp.logical_not(inner))
            def _():
                total = s.part[t % 2, half] + s.y_in[zd, half].astype(jnp.float32)
                s.outgoing[1, zd, half] = total.astype(jnp.bfloat16)

            remote(
                s.outgoing.at[1, zd, half],
                s.incoming.at[way, zd, half],
                s.z_send.at[zd, half],
                s.z_recv.at[way, zd, half],
                other,
            ).start()

    @pl.loop(0, planes + 1)
    def _(u):
        @pl.when(u < planes)
        def _():
            attend(u)

        @pl.when(u > 0)
        def _():
            project(u - 1)

        @pl.when(u > 1)
        def _():
            relay(u - 2)

    squares = 0.0
    for half in range(2):
        landed(s.y_in.at[z, half], s.y_recv.at[z, half])
        s.part[0, half] = (
            s.part[(planes - 1) % 2, half]
            + s.y_in[z, half].astype(jnp.float32)
            + residual[:, cols[half]].astype(jnp.float32)
        )
        for way, there in ((RIGHT, z > 0), (LEFT, z < planes - 1)):

            @pl.when(there)
            def _():
                from_line(z, way, half)
                s.part[0, half] = s.part[0, half] + s.incoming[way, z, half].astype(jnp.float32)

        value = s.part[0, half].astype(jnp.bfloat16)
        hidden[:, cols[half]] = value
        value = value.astype(jnp.float32)
        squares = squares + jnp.sum(value * value, axis=-1, keepdims=True)
    factor = lax.rsqrt(squares / width + epsilon)
    for half in range(2):
        value = hidden[:, cols[half]].astype(jnp.float32)
        s.normed[:, cols[half]] = (value * factor * gain[:, cols[half]]).astype(jnp.bfloat16)

    p = place_of(chip, m)

    def at(offset, c):
        return chip_at((p + offset + m) % m, m) * 2 + c

    neighbour = (at(1, core), at(-1, core))
    offsets = [0]
    for d in range(1, reach):
        offsets += [-d, d]
    offsets.append(reach)

    def forward(src, owner, way, half, d):
        send(
            src,
            s.held.at[owner, :, cols[half]],
            s.ring_send.at[way, d, half],
            s.ring_recv.at[way, d, half],
            neighbour[way],
        )

    for way, half in PAIRS:
        forward(s.normed.at[:, cols[half]], me, way, half, 0)
    send(s.normed, s.held.at[me], s.pass_send.at[0, 0, 0], s.pass_recv.at[0, 0, 0], mate)
    s.held[me] = s.normed[...]
    for t in range(planes):
        zd = target(t)
        for half in range(2):
            remote(
                s.outgoing.at[0, zd, half],
                s.y_in.at[zd, half],
                s.y_send.at[zd, half],
                s.y_recv.at[zd, half],
                across,
            ).wait_send()
            if t < planes - 1:
                remote(
                    s.outgoing.at[1, zd, half],
                    s.incoming.at[0, zd, half],
                    s.z_send.at[zd, half],
                    s.z_recv.at[0, zd, half],
                    across,
                ).wait_send()
    for c in range(m):
        remote(
            s.att.at[c, 1 - core], s.att_mate.at[c], s.mate_send.at[c], s.mate_recv.at[c], mate
        ).wait_send()
    for j in range(1, n):
        landed(s.tables.at[(me + n - j) % n], s.t_recv.at[j])

    def wait_mate(offset):
        if offset == 0:
            landed(s.held.at[mate], s.pass_recv.at[0, 0, 0])
            return
        d = abs(offset)
        for way, half in PAIRS:
            if travels(way, half, d, reach) and (d == reach or (way == RIGHT) == (offset < 0)):
                landed(
                    s.held.at[at(offset, 1 - core), :, cols[half]], s.pass_recv.at[way, d, half]
                )

    spots = lax.broadcasted_iota(jnp.int32, (places, LANES), 0).astype(jnp.float32)

    def pick(offset):
        k = offsets.index(offset)
        wait_mate(offset)
        for cc in range(2):
            owner = at(offset, cc)
            marks = []
            for e in range(local_count):
                place = s.tables[owner, pl.ds(core * local_count + e, 1), :]
                marks.append(jnp.where(spots == place, 1.0, 0.0))
            marks = jnp.concatenate(marks, axis=0)[:, :rows].astype(jnp.bfloat16)

            @pl.loop(0, width // COLUMNS_STEP)
            def _(i):
                part = pl.ds(pl.multiple_of(i * COLUMNS_STEP, COLUMNS_STEP), COLUMNS_STEP)
                picked = jnp.dot(
                    marks, s.held[owner, :, part], preferred_element_type=jnp.float32
                ).astype(jnp.bfloat16)
                for e in range(local_count):
                    s.rows_in[2 * k + cc, e, :, part] = picked[e * places : (e + 1) * places]

        owner = at(offset, core)
        shares = []
        for side in (core, 1 - core):
            for e in range(local_count):
                place = s.tables[owner, pl.ds(side * local_count + e, 1), :]
                portion = s.tables[owner, pl.ds((2 + side) * local_count + e, 1), :]
                shares.append(jnp.where(spots == place, portion, 0.0))
        shares = jnp.concatenate(shares, axis=0).T
        s.mix[k] = shares[:rows].astype(jnp.bfloat16)

    def expand(e, f, first, last):
        count = (last - first) * places
        x = s.rows_in[first:last, e].reshape(count, width)
        gate = jnp.dot(
            x, s.gate_up[e, :, f * FF_STEP : (f + 1) * FF_STEP], preferred_element_type=jnp.float32
        )
        up = jnp.dot(
            x,
            s.gate_up[e, :, ff + f * FF_STEP : ff + (f + 1) * FF_STEP],
            preferred_element_type=jnp.float32,
        )
        value = gate / (1.0 + jnp.exp(-gate)) * up
        s.active[e, first * places : last * places, f * FF_STEP : (f + 1) * FF_STEP] = value.astype(
            jnp.bfloat16
        )

    def contract(e, first, last):
        count = (last - first) * places

        @pl.loop(0, width // COLUMNS_STEP)
        def _(i):
            part = pl.ds(pl.multiple_of(i * COLUMNS_STEP, COLUMNS_STEP), COLUMNS_STEP)
            value = jnp.dot(
                s.active[e, first * places : last * places, :],
                s.down[e, :, part],
                preferred_element_type=jnp.float32,
            )
            s.rows_in[first:last, e, :, part] = value.astype(jnp.bfloat16).reshape(
                last - first, places, COLUMNS_STEP
            )

    def trade(first, last):
        for k in reversed(range(first // 2, last // 2)):
            send(
                s.rows_in.at[2 * k + 1 - core],
                s.rows_mate.at[k],
                s.trade_send.at[k],
                s.trade_recv.at[k],
                mate,
            )

    def expert_jobs(first, last):
        jobs = []
        for e in range(local_count):
            for f in range(ff // FF_STEP):
                jobs.append(functools.partial(expand, e, f, first, last))
        for e in range(local_count):
            jobs.append(functools.partial(contract, e, first, last))
        jobs.append(functools.partial(trade, first, last))
        return jobs

    early = 2 * (2 * reach - 3)
    jobs = deque()
    waits = {d: sum(travels(way, half, d, reach) for way, half in PAIRS) for d in range(1, reach + 1)}
    left = sum(waits.values())

    def level(d):
        found = [o for o in offsets if abs(o) == d]
        return [functools.partial(pick, o) for o in found]

    for d in range(1, reach + 1):
        jobs.extend(level(d - 1))
        if d == reach - 1:
            for copy in weights[1:]:
                jobs.append(copy.wait)
            jobs.extend(expert_jobs(0, early))
        for way, half in PAIRS:
            if not travels(way, half, d, reach):
                continue
            owner = at(-d if way == RIGHT else d, core)
            piece = s.held.at[owner, :, cols[half]]
            landed(piece, s.ring_recv.at[way, d - 1, half])
            if travels(way, half, d + 1, reach):
                forward(piece, owner, way, half, d)
            send(piece, piece, s.pass_send.at[way, d, half], s.pass_recv.at[way, d, half], mate)
            for _ in range(-(-len(jobs) // left)):
                jobs.popleft()()
            left -= 1
    jobs.extend(level(reach))
    while jobs:
        jobs.popleft()()
    for job in expert_jobs(early, 2 * m):
        job()

    traded = set()

    def portion(offset, half, i):
        k = offsets.index(offset)
        part = pl.ds(
            pl.multiple_of(half * half_width + i * COLUMNS_STEP, COLUMNS_STEP), COLUMNS_STEP
        )
        depth = local_count * places
        both = jnp.concatenate(
            [
                s.rows_in[2 * k + core, :, :, part].reshape(depth, COLUMNS_STEP),
                s.rows_mate[k, :, :, part].reshape(depth, COLUMNS_STEP),
            ],
            axis=0,
        )
        return jnp.dot(s.mix[k], both, preferred_element_type=jnp.float32)

    def meet(offset):
        k = offsets.index(offset)
        if k not in traded:
            landed(s.rows_mate.at[k], s.trade_recv.at[k])
            traded.add(k)

    for d in range(reach, 0, -1):
        for way, half in ((RIGHT, 1), (LEFT, 0), (RIGHT, 0), (LEFT, 1)):
            if not travels(way, half, d, reach):
                continue
            offset = d if (way == RIGHT or d == reach) else -d
            meet(offset)
            adds = travels(way, half, d + 1, reach)
            if adds:
                landed(s.incoming.at[way, d, half], s.back_recv.at[way, d, half])

            @pl.loop(0, half_width // COLUMNS_STEP)
            def _(i):
                part = pl.ds(pl.multiple_of(i * COLUMNS_STEP, COLUMNS_STEP), COLUMNS_STEP)
                total = portion(offset, half, i)
                if adds:
                    total = total + s.incoming[way, d, half, :, part].astype(jnp.float32)
                s.outgoing[way, d - 1, half, :, part] = total.astype(jnp.bfloat16)

            send(
                s.outgoing.at[way, d - 1, half],
                s.incoming.at[way, d - 1, half],
                s.back_send.at[way, d - 1, half],
                s.back_recv.at[way, d - 1, half],
                neighbour[way],
            )
    meet(0)
    for half in range(2):
        for way in (RIGHT, LEFT):
            landed(s.incoming.at[way, 0, half], s.back_recv.at[way, 0, half])

        @pl.loop(0, half_width // COLUMNS_STEP)
        def _(i):
            part = pl.ds(pl.multiple_of(i * COLUMNS_STEP, COLUMNS_STEP), COLUMNS_STEP)
            out = pl.ds(
                pl.multiple_of(half * half_width + i * COLUMNS_STEP, COLUMNS_STEP), COLUMNS_STEP
            )
            total = portion(0, half, i)
            for way in (RIGHT, LEFT):
                total = total + s.incoming[way, 0, half, :, part].astype(jnp.float32)
            result[:, out] = total.astype(jnp.bfloat16)

    finish_sends()


def local(
    n,
    queries,
    fresh_key_value,
    cache_key_value,
    residual,
    norm_gain,
    out_proj,
    w_gate_up,
    w_down,
    route_ids,
    route_weights,
    placement,
):
    rows, width = residual.shape
    experts = placement.shape[0]
    local_count, _, wide = w_gate_up.shape
    key_count = cache_key_value.shape[1]
    places = block_places(rows, experts)
    m, planes, reach = n // 2, n // 4, n // 4
    share = n // KEY_VALUE_HEADS
    head_width = QUERY_HEADS // n * HEAD_SIZE
    levels = max(1, share.bit_length() - 2)
    half = width // 2
    narrow = jnp.bfloat16
    sems = pltpu.SemaphoreType.DMA
    scratch = dict(
        kv=pltpu.VMEM((2, KEY_VALUE_HEADS, share, key_count, HEAD_SIZE), narrow),
        own=pltpu.VMEM((2, KEY_VALUE_HEADS, share, rows, HEAD_SIZE), narrow),
        q=pltpu.VMEM((n, rows, head_width), narrow),
        proj_mine=pltpu.VMEM((head_width, width), narrow),
        proj_mate=pltpu.VMEM((head_width, width), narrow),
        gate_up=pltpu.VMEM(w_gate_up.shape, narrow),
        down=pltpu.VMEM(w_down.shape, narrow),
        table=pltpu.VMEM((m, 4 * local_count, LANES), jnp.float32),
        tables=pltpu.VMEM((n, 4 * local_count, LANES), jnp.float32),
        att=pltpu.VMEM((m, 2, rows, head_width), narrow),
        att_mate=pltpu.VMEM((m, rows, head_width), narrow),
        part=pltpu.VMEM((2, 2, rows, half), jnp.float32),
        y_in=pltpu.VMEM((planes, 2, rows, half), narrow),
        outgoing=pltpu.VMEM((2, reach, 2, rows, half), narrow),
        incoming=pltpu.VMEM((2, reach, 2, rows, half), narrow),
        normed=pltpu.VMEM((rows, width), narrow),
        held=pltpu.VMEM((n, rows, width), narrow),
        rows_in=pltpu.VMEM((n, local_count, places, width), narrow),
        rows_mate=pltpu.VMEM((m, local_count, places, width), narrow),
        active=pltpu.VMEM((local_count, n * places, wide // 2), narrow),
        mix=pltpu.VMEM((m, rows, 2 * local_count * places), narrow),
        kv_send=sems((2, KEY_VALUE_HEADS)),
        kv_recv=sems((2, KEY_VALUE_HEADS)),
        fw_send=sems((2, KEY_VALUE_HEADS, levels + 1, share // 2)),
        fw_recv=sems((2, KEY_VALUE_HEADS, share)),
        q_send=sems((n,)),
        q_recv=sems((n,)),
        t_send=sems((n,)),
        t_recv=sems((n,)),
        load=sems((3,)),
        mate_send=sems((m + 1,)),
        mate_recv=sems((m + 1,)),
        y_send=sems((planes, 2)),
        y_recv=sems((planes, 2)),
        z_send=sems((planes, 2)),
        z_recv=sems((2, planes, 2)),
        ring_send=sems((2, reach, 2)),
        ring_recv=sems((2, reach, 2)),
        pass_send=sems((2, reach + 1, 2)),
        pass_recv=sems((2, reach + 1, 2)),
        trade_send=sems((m,)),
        trade_recv=sems((m,)),
        back_send=sems((2, reach, 2)),
        back_recv=sems((2, reach, 2)),
    )
    hidden, result = pl.pallas_call(
        functools.partial(whole_kernel, n, tuple(scratch)),
        out_shape=[jax.ShapeDtypeStruct((rows, width), narrow)] * 2,
        in_specs=[ANY] * 6 + [VMEM] * 5,
        out_specs=[VMEM] * 2,
        scratch_shapes=list(scratch.values()),
        compiler_params=pltpu.CompilerParams(
            collective_id=0, has_side_effects=True, vmem_limit_bytes=60 * 2**20
        ),
        name="whole",
    )(
        queries,
        fresh_key_value,
        cache_key_value,
        out_proj,
        w_gate_up,
        w_down,
        residual,
        norm_gain.reshape(1, -1),
        route_ids,
        route_weights,
        placement.reshape(1, -1),
    )
    return (hidden, result)


def solution(mesh):
    in_specs = (
        P(("groups", "ctx"), None),
        P(None, ("groups", "ctx"), None),
        P(None, ("groups", "ctx"), None),
        P(("groups", "ctx"), None),
        P(),
        P("ctx", None),
        P("ctx", None, None),
        P("ctx", None, None),
        P(("groups", "ctx"), None),
        P(("groups", "ctx"), None),
        P(),
    )
    out_specs = (P(("groups", "ctx"), None), P(("groups", "ctx"), None))
    return jax.shard_map(
        functools.partial(local, mesh.shape["ctx"]),
        mesh=mesh,
        in_specs=in_specs,
        out_specs=out_specs,
        check_vma=False,
    )
```

```python
import functools
import types
from collections import deque

import jax
import jax.numpy as jnp
from jax import lax
from jax.experimental import pallas as pl
from jax.experimental.pallas import tpu as pltpu
from jax.sharding import PartitionSpec as P

QUERY_HEADS = 32
KEY_VALUE_HEADS = 4
HEAD_SIZE = 128
TOPK = 8
COLUMNS_STEP = 512
FF_STEP = 256
LANES = 128

epsilon = 1e-06

VMEM = pl.BlockSpec(memory_space=pltpu.VMEM)
ANY = pl.BlockSpec(memory_space=pl.ANY)
RIGHT, LEFT = 0, 1
PAIRS = ((RIGHT, 0), (LEFT, 1), (RIGHT, 1), (LEFT, 0))


def chip_at(q, m):
    return jnp.where(q < m // 2, 2 * q, 2 * (m - 1 - q) + 1)


def place_of(chip, m):
    return jnp.where(chip % 2 == 0, chip // 2, m - 1 - chip // 2)


def flip(value, key, size):
    total, bit = 0, 1
    while bit < size:
        total = total + (value // bit + key // bit) % 2 * bit
        bit *= 2
    return total


def greet(others):
    barrier = pltpu.get_barrier_semaphore()
    for other in others:
        pl.semaphore_signal(
            barrier, inc=1, device_id={"ctx": other}, device_id_type=pl.DeviceIdType.MESH
        )
    pl.semaphore_wait(barrier, len(others))


def remote(src, dst, send, recv, other):
    return pltpu.make_async_remote_copy(
        src_ref=src,
        dst_ref=dst,
        send_sem=send,
        recv_sem=recv,
        device_id={"ctx": other},
        device_id_type=pl.DeviceIdType.MESH,
    )


def landed(piece, sem):
    pltpu.make_async_copy(piece, piece, sem).wait()


def travels(way, half, d, reach):
    return d < reach or (d == reach and half == way)


def block_places(rows, experts):
    most = max(2, 3 * rows * TOPK // (2 * experts))
    return -(-most // 16) * 16


def whole_kernel(
    n,
    names,
    queries,
    fresh,
    cache,
    proj,
    gate_up,
    down,
    residual,
    gain,
    ids,
    route,
    placement,
    hidden,
    result,
    *scratch,
):
    s = types.SimpleNamespace(**dict(zip(names, scratch)))
    m, planes, reach = n // 2, n // 4, n // 4
    rows, width = residual.shape
    half_width = width // 2
    cols = [pl.ds(h * half_width, half_width) for h in range(2)]
    local_count, _, wide = gate_up.shape
    ff = wide // 2
    experts = placement.shape[1]
    places = s.rows_in.shape[2]
    per = QUERY_HEADS // n
    head_width = per * HEAD_SIZE
    share = n // KEY_VALUE_HEADS

    me = lax.axis_index("ctx")
    core, chip = me % 2, me // 2
    y, z = chip % 2, chip // 2

    def device(zz, yy, cc):
        return (zz * 2 + yy) * 2 + cc

    mate = device(z, y, 1 - core)
    across = device(z, 1 - y, core)
    started = []

    def send(src, dst, send_sem, recv_sem, other):
        copy = remote(src, dst, send_sem, recv_sem, other)
        copy.start()
        started.append(copy)

    def finish_sends():
        while started:
            started.pop(0).wait_send()

    greet([(me + j) % n for j in range(1, n)])

    mine, rank = me // share, me % share
    sources = ((cache, s.kv), (fresh, s.own))

    def lanes_of(head):
        return pl.ds(pl.multiple_of(head * HEAD_SIZE, HEAD_SIZE), HEAD_SIZE)

    local = []
    for kind, (src, dst) in enumerate(sources):
        copy = pltpu.make_async_copy(
            src.at[:, :, lanes_of(mine)], dst.at[:, mine, rank], s.kv_recv.at[kind, 0]
        )
        copy.start()
        local.append(copy)

    def spread_kv(kind):
        src, dst = sources[kind]
        for i in range(1, KEY_VALUE_HEADS):
            head = (mine + i) % KEY_VALUE_HEADS
            send(
                src.at[:, :, lanes_of(head)],
                dst.at[:, mine, rank],
                s.kv_send.at[kind, i],
                s.kv_recv.at[kind, i],
                head * share + rank,
            )

    spread_kv(0)
    spread_kv(1)

    copy = pltpu.make_async_copy(
        queries.at[:, pl.ds(pl.multiple_of(me * head_width, LANES), head_width)],
        s.q.at[me],
        s.q_recv.at[me],
    )
    copy.start()

    def send_queries(key, start=True):
        for dy in (1, 0):
            for dc in (0, 1):
                if (key, dy, dc) == (0, 0, 0):
                    continue
                other = device(flip(z, key, planes), (y + dy) % 2, (core + dc) % 2)
                copy = remote(
                    queries.at[:, pl.ds(pl.multiple_of(other * head_width, LANES), head_width)],
                    s.q.at[me],
                    s.q_send.at[key * 4 + dy * 2 + dc],
                    s.q_recv.at[me],
                    other,
                )
                if start:
                    copy.start()
                else:
                    copy.wait_send()

    send_queries(0)
    send(proj, s.proj_mate, s.mate_send.at[m], s.mate_recv.at[m], mate)
    weights = [
        pltpu.make_async_copy(proj, s.proj_mine, s.load.at[0]),
        pltpu.make_async_copy(gate_up, s.gate_up, s.load.at[1]),
        pltpu.make_async_copy(down, s.down, s.load.at[2]),
    ]
    for copy in weights:
        copy.start()

    scores = route[...]
    scores = scores / jnp.sum(scores, axis=0, keepdims=True)
    listed = lax.broadcasted_iota(jnp.int32, (experts, rows), 0)
    by_expert = jnp.zeros((experts, rows), jnp.float32)
    for k in range(TOPK):
        by_expert = by_expert + jnp.where(listed == ids[k : k + 1], scores[k : k + 1], 0.0)
    by_expert = jnp.concatenate(
        [by_expert, jnp.zeros((experts, LANES - rows), jnp.float32)], axis=1
    ).astype(jnp.bfloat16)
    moved = jnp.where(
        lax.broadcasted_iota(jnp.int32, (experts, experts), 0) == placement[...], 1.0, 0.0
    ).astype(jnp.bfloat16)
    by_slot = jnp.dot(moved, by_expert, preferred_element_type=jnp.float32)
    named = jnp.where(by_slot > 0, 1.0, 0.0)
    before = jnp.where(
        lax.broadcasted_iota(jnp.int32, (LANES, LANES), 0)
        < lax.broadcasted_iota(jnp.int32, (LANES, LANES), 1),
        1.0,
        0.0,
    ).astype(jnp.bfloat16)
    ranks = jnp.dot(named.astype(jnp.bfloat16), before, preferred_element_type=jnp.float32)
    ranks = jnp.where(by_slot > 0, ranks, -1.0)
    pair = 2 * local_count
    for c in range(m):
        s.table[c, 0:pair, :] = ranks[c * pair : (c + 1) * pair]
        s.table[c, pair : 2 * pair, :] = by_slot[c * pair : (c + 1) * pair]
    s.tables[me] = s.table[chip]
    for j in range(1, n):
        other = (me + j) % n
        send(
            s.table.at[other // 2], s.tables.at[me], s.t_send.at[j], s.t_recv.at[j], other
        )

    steps = []
    bit = 2
    while bit < share:
        steps.append(bit)
        bit *= 2

    outer = jnp.logical_or(z < planes // 4, z >= planes - planes // 4)

    def send_far():
        for key in range(planes - 1, planes // 2 - 1, -1):
            send_queries(key)

    for kind in range(2):
        dst = sources[kind][1]

        def slot(g, r, dst=dst):
            return dst.at[:, g, r]

        local[kind].wait()
        order = [(mine + KEY_VALUE_HEADS - i) % KEY_VALUE_HEADS for i in range(KEY_VALUE_HEADS)]
        held = [0]
        for number, bit in enumerate(steps):
            for i, g in enumerate(order):
                if number == 0 and i > 0:
                    landed(slot(g, rank), s.kv_recv.at[kind, i])
                for k in held:
                    send(
                        slot(g, flip(rank, k, share)),
                        slot(g, flip(rank, k, share)),
                        s.fw_send.at[kind, i, number, k // 2],
                        s.fw_recv.at[kind, i, k + bit],
                        mine * share + flip(rank, bit, share),
                    )
            for i, g in enumerate(order):
                for k in held:
                    landed(slot(g, flip(rank, k + bit, share)), s.fw_recv.at[kind, i, k + bit])
                    if number == len(steps) - 1:
                        send(
                            slot(g, flip(rank, k + bit, share)),
                            slot(g, flip(rank, k + bit, share)),
                            s.fw_send.at[kind, i, len(steps), (k + bit) // 2],
                            s.fw_recv.at[kind, i, k + bit + 1],
                            mate,
                        )
                    if number == len(steps) - 1:
                        send(
                            slot(g, flip(rank, k, share)),
                            slot(g, flip(rank, k, share)),
                            s.fw_send.at[kind, i, len(steps), k // 2],
                            s.fw_recv.at[kind, i, k + 1],
                            mate,
                        )
            held = held + [k + bit for k in held]
        if kind == 0:
            pl.when(outer)(send_far)
    for kind in range(2):
        dst = sources[kind][1]
        for i in range(KEY_VALUE_HEADS):
            g = (mine + KEY_VALUE_HEADS - i) % KEY_VALUE_HEADS
            for k in range(0, share, 2):
                landed(dst.at[:, g, flip(rank, k + 1, share)], s.fw_recv.at[kind, i, k + 1])
    landed(s.proj_mate, s.mate_recv.at[m])
    weights[0].wait()

    key_count = s.kv.shape[3]
    scale = HEAD_SIZE ** (-0.5)

    def target(t):
        turn, above = t - 1, planes - 1 - z
        rising = jnp.where(turn < above, planes - 1 - turn, turn - above)
        falling = jnp.where(turn < z, turn, planes - 1 - (turn - z))
        return jnp.where(t == 0, z, jnp.where(z < planes // 2, rising, falling))

    def attend(t):
        @pl.loop(0, 2)
        def _(line):
            c = target(t) * 2 + (y + 1 + line) % 2
            for cc in range(2):
                landed(s.q.at[2 * c + cc], s.q_recv.at[2 * c + cc])
            keys = s.kv[0].reshape(n * key_count, HEAD_SIZE)
            values = s.kv[1].reshape(n * key_count, HEAD_SIZE)
            fresh_key = s.own[0, (2 * c) // share, pl.ds((2 * c) % share, 2)]
            fresh_key = fresh_key.reshape(2 * rows, HEAD_SIZE).astype(jnp.float32)
            fresh_value = s.own[1, (2 * c) // share, pl.ds((2 * c) % share, 2)]
            fresh_value = fresh_value.reshape(2 * rows, HEAD_SIZE).astype(jnp.float32)
            for h in range(per):
                lanes = slice(h * HEAD_SIZE, (h + 1) * HEAD_SIZE)
                q = s.q[pl.ds(2 * c, 2), :, lanes].reshape(2 * rows, HEAD_SIZE)
                scores = lax.dot_general(
                    q, keys, (((1,), (1,)), ((), ())), preferred_element_type=jnp.float32
                )
                own = jnp.sum(q.astype(jnp.float32) * fresh_key, axis=-1, keepdims=True)
                peak = jnp.maximum(own, jnp.max(scores, axis=-1, keepdims=True))
                weight = jnp.exp((scores - peak) * scale)
                own = jnp.exp((own - peak) * scale)
                total = jnp.sum(weight, axis=-1, keepdims=True) + own
                mixed = jnp.dot(
                    weight.astype(jnp.bfloat16), values, preferred_element_type=jnp.float32
                )
                mixed = (mixed + own * fresh_value) / total
                s.att[c, :, :, lanes] = mixed.astype(jnp.bfloat16).reshape(2, rows, HEAD_SIZE)
            remote(
                s.att.at[c, 1 - core],
                s.att_mate.at[c],
                s.mate_send.at[c],
                s.mate_recv.at[c],
                mate,
            ).start()

    def project(t):
        zd = target(t)
        chips = [zd * 2 + (1 - y), zd * 2 + y]
        for c in chips:
            landed(s.att_mate.at[c], s.mate_recv.at[c])
        left = jnp.concatenate([s.att[c, core] for c in chips], axis=0)
        left_mate = jnp.concatenate([s.att_mate[c] for c in chips], axis=0)
        for half in range(2):

            @pl.loop(0, half_width // COLUMNS_STEP)
            def _(i):
                part = pl.ds(pl.multiple_of(i * COLUMNS_STEP, COLUMNS_STEP), COLUMNS_STEP)
                at = pl.ds(
                    pl.multiple_of(half * half_width + i * COLUMNS_STEP, COLUMNS_STEP), COLUMNS_STEP
                )
                product = jnp.dot(
                    left, s.proj_mine[:, at], preferred_element_type=jnp.float32
                ) + jnp.dot(left_mate, s.proj_mate[:, at], preferred_element_type=jnp.float32)
                s.outgoing[0, zd, half, :, part] = product[:rows].astype(jnp.bfloat16)
                s.outgoing[1, zd, half, :, part] = product[rows:].astype(jnp.bfloat16)

            remote(
                s.outgoing.at[0, zd, half],
                s.y_in.at[zd, half],
                s.y_send.at[zd, half],
                s.y_recv.at[zd, half],
                across,
            ).start()

    def from_line(zd, way, half):
        landed(s.incoming.at[way, zd, half], s.z_recv.at[way, zd, half])

    def relay(t):
        zd = target(t)
        way = jnp.where(zd > z, RIGHT, LEFT)
        inner = jnp.where(zd > z, z > 0, z < planes - 1)
        other = device(jnp.where(zd > z, z + 1, z - 1), y, core)
        for half in range(2):
            landed(s.y_in.at[zd, half], s.y_recv.at[zd, half])

            @pl.when(inner)
            def _():
                from_line(zd, way, half)
                total = (
                    s.outgoing[1, zd, half].astype(jnp.float32)
                    + s.y_in[zd, half].astype(jnp.float32)
                    + s.incoming[way, zd, half].astype(jnp.float32)
                )
                s.outgoing[1, zd, half] = total.astype(jnp.bfloat16)

            @pl.when(jnp.logical_not(inner))
            def _():
                total = s.outgoing[1, zd, half].astype(jnp.float32) + s.y_in[zd, half].astype(
                    jnp.float32
                )
                s.outgoing[1, zd, half] = total.astype(jnp.bfloat16)

            remote(
                s.outgoing.at[1, zd, half],
                s.incoming.at[way, zd, half],
                s.z_send.at[zd, half],
                s.z_recv.at[way, zd, half],
                other,
            ).start()

    pl.when(jnp.logical_not(outer))(send_far)

    @pl.loop(0, planes + 2)
    def _(u):
        @pl.when(u < planes)
        def _():
            attend(u)

        @pl.when(u == 0)
        def _():
            for key in range(planes // 2 - 1, 0, -1):
                send_queries(key)

        @pl.when(u < planes)
        def _():
            project(u)

        early = jnp.logical_and(outer, jnp.logical_and(u > 1, u <= planes))

        @pl.when(early)
        def _():
            relay(u - 1)

        @pl.when(jnp.logical_and(jnp.logical_not(outer), u > 2))
        def _():
            relay(u - 2)

    squares = 0.0
    for half in range(2):
        landed(s.y_in.at[z, half], s.y_recv.at[z, half])
        s.part[half] = (
            s.outgoing[1, z, half].astype(jnp.float32)
            + s.y_in[z, half].astype(jnp.float32)
            + residual[:, cols[half]].astype(jnp.float32)
        )
        for way, there in ((RIGHT, z > 0), (LEFT, z < planes - 1)):

            @pl.when(there)
            def _():
                from_line(z, way, half)
                s.part[half] = s.part[half] + s.incoming[way, z, half].astype(jnp.float32)

        value = s.part[half].astype(jnp.bfloat16)
        hidden[:, cols[half]] = value
        value = value.astype(jnp.float32)
        squares = squares + jnp.sum(value * value, axis=-1, keepdims=True)
    factor = lax.rsqrt(squares / width + epsilon)
    for half in range(2):
        value = hidden[:, cols[half]].astype(jnp.float32)
        s.normed[:, cols[half]] = (value * factor * gain[:, cols[half]]).astype(jnp.bfloat16)

    p = place_of(chip, m)

    def at(offset, c):
        return chip_at((p + offset + m) % m, m) * 2 + c

    neighbour = (at(1, core), at(-1, core))
    offsets = [0]
    for d in range(1, reach):
        offsets += [-d, d]
    offsets.append(reach)

    def forward(src, owner, way, half, d):
        send(
            src,
            s.held.at[owner, :, cols[half]],
            s.ring_send.at[way, d, half],
            s.ring_recv.at[way, d, half],
            neighbour[way],
        )

    for way, half in PAIRS:
        forward(s.normed.at[:, cols[half]], me, way, half, 0)
    send(s.normed, s.held.at[me], s.pass_send.at[0, 0, 0], s.pass_recv.at[0, 0, 0], mate)
    s.held[me] = s.normed[...]
    for key in range(planes):
        zd = flip(z, key, planes)
        for half in range(2):
            remote(
                s.outgoing.at[0, zd, half],
                s.y_in.at[zd, half],
                s.y_send.at[zd, half],
                s.y_recv.at[zd, half],
                across,
            ).wait_send()
            if key > 0:
                remote(
                    s.outgoing.at[1, zd, half],
                    s.incoming.at[0, zd, half],
                    s.z_send.at[zd, half],
                    s.z_recv.at[0, zd, half],
                    across,
                ).wait_send()
    for c in range(m):
        remote(
            s.att.at[c, 1 - core], s.att_mate.at[c], s.mate_send.at[c], s.mate_recv.at[c], mate
        ).wait_send()
    for key in range(planes):
        send_queries(key, start=False)
    for j in range(1, n):
        landed(s.tables.at[(me + n - j) % n], s.t_recv.at[j])

    def wait_mate(offset):
        if offset == 0:
            landed(s.held.at[mate], s.pass_recv.at[0, 0, 0])
            return
        d = abs(offset)
        for way, half in PAIRS:
            if travels(way, half, d, reach) and (d == reach or (way == RIGHT) == (offset < 0)):
                landed(
                    s.held.at[at(offset, 1 - core), :, cols[half]], s.pass_recv.at[way, d, half]
                )

    spots = lax.broadcasted_iota(jnp.int32, (places, LANES), 0).astype(jnp.float32)

    def pick(offset):
        k = offsets.index(offset)
        wait_mate(offset)
        for cc in range(2):
            owner = at(offset, cc)
            marks = []
            for e in range(local_count):
                place = s.tables[owner, pl.ds(core * local_count + e, 1), :]
                marks.append(jnp.where(spots == place, 1.0, 0.0))
            marks = jnp.concatenate(marks, axis=0)[:, :rows].astype(jnp.bfloat16)

            @pl.loop(0, width // COLUMNS_STEP)
            def _(i):
                part = pl.ds(pl.multiple_of(i * COLUMNS_STEP, COLUMNS_STEP), COLUMNS_STEP)
                picked = jnp.dot(
                    marks, s.held[owner, :, part], preferred_element_type=jnp.float32
                ).astype(jnp.bfloat16)
                for e in range(local_count):
                    s.rows_in[2 * k + cc, e, :, part] = picked[e * places : (e + 1) * places]

        owner = at(offset, core)
        shares = []
        for side in (core, 1 - core):
            for e in range(local_count):
                place = s.tables[owner, pl.ds(side * local_count + e, 1), :]
                portion = s.tables[owner, pl.ds((2 + side) * local_count + e, 1), :]
                shares.append(jnp.where(spots == place, portion, 0.0))
        shares = jnp.concatenate(shares, axis=0).T
        s.mix[k] = shares[:rows].astype(jnp.bfloat16)

    def expand(e, f, first, last):
        count = (last - first) * places
        x = s.rows_in[first:last, e].reshape(count, width)
        gate = jnp.dot(
            x, s.gate_up[e, :, f * FF_STEP : (f + 1) * FF_STEP], preferred_element_type=jnp.float32
        )
        up = jnp.dot(
            x,
            s.gate_up[e, :, ff + f * FF_STEP : ff + (f + 1) * FF_STEP],
            preferred_element_type=jnp.float32,
        )
        value = gate / (1.0 + jnp.exp(-gate)) * up
        s.active[e, first * places : last * places, f * FF_STEP : (f + 1) * FF_STEP] = value.astype(
            jnp.bfloat16
        )

    def contract(e, first, last):
        count = (last - first) * places

        @pl.loop(0, width // COLUMNS_STEP)
        def _(i):
            part = pl.ds(pl.multiple_of(i * COLUMNS_STEP, COLUMNS_STEP), COLUMNS_STEP)
            value = jnp.dot(
                s.active[e, first * places : last * places, :],
                s.down[e, :, part],
                preferred_element_type=jnp.float32,
            )
            s.rows_in[first:last, e, :, part] = value.astype(jnp.bfloat16).reshape(
                last - first, places, COLUMNS_STEP
            )

    def trade(first, last):
        for k in reversed(range(first // 2, last // 2)):
            send(
                s.rows_in.at[2 * k + 1 - core],
                s.rows_mate.at[k],
                s.trade_send.at[k],
                s.trade_recv.at[k],
                mate,
            )

    def expert_jobs(first, last):
        jobs = []
        for e in range(local_count):
            for f in range(ff // FF_STEP):
                jobs.append(functools.partial(expand, e, f, first, last))
        for e in range(local_count):
            jobs.append(functools.partial(contract, e, first, last))
        jobs.append(functools.partial(trade, first, last))
        return jobs

    early = 2 * (2 * reach - 3)
    jobs = deque()
    waits = {d: sum(travels(way, half, d, reach) for way, half in PAIRS) for d in range(1, reach + 1)}
    left = sum(waits.values())

    def level(d):
        found = [o for o in offsets if abs(o) == d]
        return [functools.partial(pick, o) for o in found]

    for d in range(1, reach + 1):
        jobs.extend(level(d - 1))
        if d == reach - 1:
            for copy in weights[1:]:
                jobs.append(copy.wait)
            jobs.extend(expert_jobs(0, early))
        for way, half in PAIRS:
            if not travels(way, half, d, reach):
                continue
            owner = at(-d if way == RIGHT else d, core)
            piece = s.held.at[owner, :, cols[half]]
            landed(piece, s.ring_recv.at[way, d - 1, half])
            if travels(way, half, d + 1, reach):
                forward(piece, owner, way, half, d)
            send(piece, piece, s.pass_send.at[way, d, half], s.pass_recv.at[way, d, half], mate)
            for _ in range(-(-len(jobs) // left)):
                jobs.popleft()()
            left -= 1
    jobs.extend(level(reach))
    while jobs:
        jobs.popleft()()
    for job in expert_jobs(early, 2 * m):
        job()

    traded = set()

    def portion(offset, half, i):
        k = offsets.index(offset)
        part = pl.ds(
            pl.multiple_of(half * half_width + i * COLUMNS_STEP, COLUMNS_STEP), COLUMNS_STEP
        )
        depth = local_count * places
        both = jnp.concatenate(
            [
                s.rows_in[2 * k + core, :, :, part].reshape(depth, COLUMNS_STEP),
                s.rows_mate[k, :, :, part].reshape(depth, COLUMNS_STEP),
            ],
            axis=0,
        )
        return jnp.dot(s.mix[k], both, preferred_element_type=jnp.float32)

    def meet(offset):
        k = offsets.index(offset)
        if k not in traded:
            landed(s.rows_mate.at[k], s.trade_recv.at[k])
            traded.add(k)

    for d in range(reach, 0, -1):
        for way, half in ((RIGHT, 1), (LEFT, 0), (RIGHT, 0), (LEFT, 1)):
            if not travels(way, half, d, reach):
                continue
            offset = d if (way == RIGHT or d == reach) else -d
            meet(offset)
            adds = travels(way, half, d + 1, reach)
            if adds:
                landed(s.incoming.at[way, d, half], s.back_recv.at[way, d, half])

            @pl.loop(0, half_width // COLUMNS_STEP)
            def _(i):
                part = pl.ds(pl.multiple_of(i * COLUMNS_STEP, COLUMNS_STEP), COLUMNS_STEP)
                total = portion(offset, half, i)
                if adds:
                    total = total + s.incoming[way, d, half, :, part].astype(jnp.float32)
                s.outgoing[way, d - 1, half, :, part] = total.astype(jnp.bfloat16)

            send(
                s.outgoing.at[way, d - 1, half],
                s.incoming.at[way, d - 1, half],
                s.back_send.at[way, d - 1, half],
                s.back_recv.at[way, d - 1, half],
                neighbour[way],
            )
    meet(0)
    for half in range(2):
        for way in (RIGHT, LEFT):
            landed(s.incoming.at[way, 0, half], s.back_recv.at[way, 0, half])

        @pl.loop(0, half_width // COLUMNS_STEP)
        def _(i):
            part = pl.ds(pl.multiple_of(i * COLUMNS_STEP, COLUMNS_STEP), COLUMNS_STEP)
            out = pl.ds(
                pl.multiple_of(half * half_width + i * COLUMNS_STEP, COLUMNS_STEP), COLUMNS_STEP
            )
            total = portion(0, half, i)
            for way in (RIGHT, LEFT):
                total = total + s.incoming[way, 0, half, :, part].astype(jnp.float32)
            result[:, out] = total.astype(jnp.bfloat16)

    finish_sends()


def keep_kernel(hidden, result, hidden_out, result_out):
    hidden_out[...] = hidden[...]
    result_out[...] = result[...]


def local(
    n,
    queries,
    fresh_key_value,
    cache_key_value,
    residual,
    norm_gain,
    out_proj,
    w_gate_up,
    w_down,
    route_ids,
    route_weights,
    placement,
):
    rows, width = residual.shape
    experts = placement.shape[0]
    local_count, _, wide = w_gate_up.shape
    key_count = cache_key_value.shape[1]
    places = block_places(rows, experts)
    m, planes, reach = n // 2, n // 4, n // 4
    share = n // KEY_VALUE_HEADS
    head_width = QUERY_HEADS // n * HEAD_SIZE
    levels = max(1, share.bit_length() - 2)
    half = width // 2
    narrow = jnp.bfloat16
    sems = pltpu.SemaphoreType.DMA
    scratch = dict(
        kv=pltpu.VMEM((2, KEY_VALUE_HEADS, share, key_count, HEAD_SIZE), narrow),
        own=pltpu.VMEM((2, KEY_VALUE_HEADS, share, rows, HEAD_SIZE), narrow),
        q=pltpu.VMEM((n, rows, head_width), narrow),
        proj_mine=pltpu.VMEM((head_width, width), narrow),
        proj_mate=pltpu.VMEM((head_width, width), narrow),
        gate_up=pltpu.VMEM(w_gate_up.shape, narrow),
        down=pltpu.VMEM(w_down.shape, narrow),
        table=pltpu.VMEM((m, 4 * local_count, LANES), jnp.float32),
        tables=pltpu.VMEM((n, 4 * local_count, LANES), jnp.float32),
        att=pltpu.VMEM((m, 2, rows, head_width), narrow),
        att_mate=pltpu.VMEM((m, rows, head_width), narrow),
        part=pltpu.VMEM((2, rows, half), jnp.float32),
        y_in=pltpu.VMEM((planes, 2, rows, half), narrow),
        outgoing=pltpu.VMEM((2, reach, 2, rows, half), narrow),
        incoming=pltpu.VMEM((2, reach, 2, rows, half), narrow),
        normed=pltpu.VMEM((rows, width), narrow),
        held=pltpu.VMEM((n, rows, width), narrow),
        rows_in=pltpu.VMEM((n, local_count, places, width), narrow),
        rows_mate=pltpu.VMEM((m, local_count, places, width), narrow),
        active=pltpu.VMEM((local_count, n * places, wide // 2), narrow),
        mix=pltpu.VMEM((m, rows, 2 * local_count * places), narrow),
        kv_send=sems((2, KEY_VALUE_HEADS)),
        kv_recv=sems((2, KEY_VALUE_HEADS)),
        fw_send=sems((2, KEY_VALUE_HEADS, levels + 1, share // 2)),
        fw_recv=sems((2, KEY_VALUE_HEADS, share)),
        q_send=sems((n,)),
        q_recv=sems((n,)),
        t_send=sems((n,)),
        t_recv=sems((n,)),
        load=sems((3,)),
        mate_send=sems((m + 1,)),
        mate_recv=sems((m + 1,)),
        y_send=sems((planes, 2)),
        y_recv=sems((planes, 2)),
        z_send=sems((planes, 2)),
        z_recv=sems((2, planes, 2)),
        ring_send=sems((2, reach, 2)),
        ring_recv=sems((2, reach, 2)),
        pass_send=sems((2, reach + 1, 2)),
        pass_recv=sems((2, reach + 1, 2)),
        trade_send=sems((m,)),
        trade_recv=sems((m,)),
        back_send=sems((2, reach, 2)),
        back_recv=sems((2, reach, 2)),
    )
    hidden, result = pl.pallas_call(
        functools.partial(whole_kernel, n, tuple(scratch)),
        out_shape=[jax.ShapeDtypeStruct((rows, width), narrow)] * 2,
        in_specs=[ANY] * 6 + [VMEM] * 5,
        out_specs=[VMEM] * 2,
        scratch_shapes=list(scratch.values()),
        compiler_params=pltpu.CompilerParams(
            collective_id=0, has_side_effects=True, vmem_limit_bytes=60 * 2**20
        ),
        name="whole",
    )(
        queries,
        fresh_key_value,
        cache_key_value,
        out_proj,
        w_gate_up,
        w_down,
        residual,
        norm_gain.reshape(1, -1),
        route_ids.T,
        route_weights.T,
        placement.reshape(1, -1),
    )
    return pl.pallas_call(
        keep_kernel,
        out_shape=[jax.ShapeDtypeStruct((rows, width), narrow)] * 2,
        in_specs=[VMEM] * 2,
        out_specs=[VMEM] * 2,
        name="keep",
    )(hidden, result)


def solution(mesh):
    in_specs = (
        P(("groups", "ctx"), None),
        P(None, ("groups", "ctx"), None),
        P(None, ("groups", "ctx"), None),
        P(("groups", "ctx"), None),
        P(),
        P("ctx", None),
        P("ctx", None, None),
        P("ctx", None, None),
        P(("groups", "ctx"), None),
        P(("groups", "ctx"), None),
        P(),
    )
    out_specs = (P(("groups", "ctx"), None), P(("groups", "ctx"), None))
    return jax.shard_map(
        functools.partial(local, mesh.shape["ctx"]),
        mesh=mesh,
        in_specs=in_specs,
        out_specs=out_specs,
        check_vma=False,
    )
```

```python
import functools
import types
from collections import deque

import jax
import jax.numpy as jnp
from jax import lax
from jax.experimental import pallas as pl
from jax.experimental.pallas import tpu as pltpu
from jax.sharding import PartitionSpec as P

QUERY_HEADS = 32
KEY_VALUE_HEADS = 4
HEAD_SIZE = 128
TOPK = 8
COLUMNS_STEP = 1024
FF_STEP = 256
LANES = 128

epsilon = 1e-06

VMEM = pl.BlockSpec(memory_space=pltpu.VMEM)
ANY = pl.BlockSpec(memory_space=pl.ANY)
RIGHT, LEFT = 0, 1
PAIRS = ((RIGHT, 0), (LEFT, 1), (RIGHT, 1), (LEFT, 0))


def chip_at(q, m):
    return jnp.where(q < m // 2, 2 * q, 2 * (m - 1 - q) + 1)


def place_of(chip, m):
    return jnp.where(chip % 2 == 0, chip // 2, m - 1 - chip // 2)


def flip(value, key, size):
    total, bit = 0, 1
    while bit < size:
        total = total + (value // bit + key // bit) % 2 * bit
        bit *= 2
    return total


def greet(others):
    barrier = pltpu.get_barrier_semaphore()
    for other in others:
        pl.semaphore_signal(
            barrier, inc=1, device_id={"ctx": other}, device_id_type=pl.DeviceIdType.MESH
        )
    pl.semaphore_wait(barrier, len(others))


def remote(src, dst, send, recv, other):
    return pltpu.make_async_remote_copy(
        src_ref=src,
        dst_ref=dst,
        send_sem=send,
        recv_sem=recv,
        device_id={"ctx": other},
        device_id_type=pl.DeviceIdType.MESH,
    )


def landed(piece, sem):
    pltpu.make_async_copy(piece, piece, sem).wait()


def travels(way, half, d, reach):
    return d < reach or (d == reach and half == way)


def block_places(rows, experts):
    most = max(2, 3 * rows * TOPK // (2 * experts))
    return -(-most // 16) * 16


def whole_kernel(
    n,
    names,
    queries,
    fresh,
    cache,
    proj,
    gate_up,
    down,
    residual,
    gain,
    ids,
    route,
    placement,
    hidden,
    result,
    *scratch,
):
    s = types.SimpleNamespace(**dict(zip(names, scratch)))
    m, planes, reach = n // 2, n // 4, n // 4
    rows, width = residual.shape
    half_width = width // 2
    cols = [pl.ds(h * half_width, half_width) for h in range(2)]
    local_count, _, wide = gate_up.shape
    ff = wide // 2
    experts = placement.shape[1]
    places = s.rows_in.shape[2]
    per = QUERY_HEADS // n
    head_width = per * HEAD_SIZE
    share = n // KEY_VALUE_HEADS

    me = lax.axis_index("ctx")
    core, chip = me % 2, me // 2
    y, z = chip % 2, chip // 2

    def device(zz, yy, cc):
        return (zz * 2 + yy) * 2 + cc

    mate = device(z, y, 1 - core)
    across = device(z, 1 - y, core)
    started = []

    def send(src, dst, send_sem, recv_sem, other):
        copy = remote(src, dst, send_sem, recv_sem, other)
        copy.start()
        started.append(copy)

    def finish_sends():
        while started:
            started.pop(0).wait_send()

    greet([(me + j) % n for j in range(1, n)])

    mine, rank = me // share, me % share
    sources = ((cache, s.kv), (fresh, s.own))

    def lanes_of(head):
        return pl.ds(pl.multiple_of(head * HEAD_SIZE, HEAD_SIZE), HEAD_SIZE)

    local = []
    for kind, (src, dst) in enumerate(sources):
        copy = pltpu.make_async_copy(
            src.at[:, :, lanes_of(mine)], dst.at[:, mine, rank], s.kv_recv.at[kind, 0]
        )
        copy.start()
        local.append(copy)

    def spread_kv(kind):
        src, dst = sources[kind]
        for i in range(1, KEY_VALUE_HEADS):
            head = (mine + i) % KEY_VALUE_HEADS
            send(
                src.at[:, :, lanes_of(head)],
                dst.at[:, mine, rank],
                s.kv_send.at[kind, i],
                s.kv_recv.at[kind, i],
                head * share + rank,
            )

    spread_kv(0)
    spread_kv(1)

    copy = pltpu.make_async_copy(
        queries.at[:, pl.ds(pl.multiple_of(me * head_width, LANES), head_width)],
        s.q.at[me],
        s.q_recv.at[me],
    )
    copy.start()

    def send_queries(key, start=True):
        for dy in (1, 0):
            for dc in (0, 1):
                if (key, dy, dc) == (0, 0, 0):
                    continue
                other = device(flip(z, key, planes), (y + dy) % 2, (core + dc) % 2)
                copy = remote(
                    queries.at[:, pl.ds(pl.multiple_of(other * head_width, LANES), head_width)],
                    s.q.at[me],
                    s.q_send.at[key * 4 + dy * 2 + dc],
                    s.q_recv.at[me],
                    other,
                )
                if start:
                    copy.start()
                else:
                    copy.wait_send()

    send_queries(0)
    send(proj, s.proj_mate, s.mate_send.at[m], s.mate_recv.at[m], mate)
    weights = [
        pltpu.make_async_copy(proj, s.proj_mine, s.load.at[0]),
        pltpu.make_async_copy(gate_up, s.gate_up, s.load.at[1]),
        pltpu.make_async_copy(down, s.down, s.load.at[2]),
    ]
    for copy in weights:
        copy.start()

    def table_copy(j):
        other = (me + j) % n
        return remote(
            s.table.at[other // 2], s.tables.at[me], s.t_send.at[j], s.t_recv.at[j], other
        )

    def fill_tables():
        scores = route[...]
        scores = scores / jnp.sum(scores, axis=0, keepdims=True)
        listed = lax.broadcasted_iota(jnp.int32, (experts, rows), 0)
        by_expert = jnp.zeros((experts, rows), jnp.float32)
        for k in range(TOPK):
            by_expert = by_expert + jnp.where(listed == ids[k : k + 1], scores[k : k + 1], 0.0)
        by_expert = jnp.concatenate(
            [by_expert, jnp.zeros((experts, LANES - rows), jnp.float32)], axis=1
        ).astype(jnp.bfloat16)
        moved = jnp.where(
            lax.broadcasted_iota(jnp.int32, (experts, experts), 0) == placement[...], 1.0, 0.0
        ).astype(jnp.bfloat16)
        by_slot = jnp.dot(moved, by_expert, preferred_element_type=jnp.float32)
        named = jnp.where(by_slot > 0, 1.0, 0.0)
        before = jnp.where(
            lax.broadcasted_iota(jnp.int32, (LANES, LANES), 0)
            < lax.broadcasted_iota(jnp.int32, (LANES, LANES), 1),
            1.0,
            0.0,
        ).astype(jnp.bfloat16)
        ranks = jnp.dot(named.astype(jnp.bfloat16), before, preferred_element_type=jnp.float32)
        ranks = jnp.where(by_slot > 0, ranks, -1.0)
        pair = 2 * local_count
        for c in range(m):
            s.table[c, 0:pair, :] = ranks[c * pair : (c + 1) * pair]
            s.table[c, pair : 2 * pair, :] = by_slot[c * pair : (c + 1) * pair]
        s.tables[me] = s.table[chip]
        for j in range(1, n):
            table_copy(j).start()

    steps = []
    bit = 2
    while bit < share:
        steps.append(bit)
        bit *= 2
    final = len(steps)
    groups = tuple(range(KEY_VALUE_HEADS))
    outer = jnp.logical_or(z < planes // 4, z >= planes - planes // 4)

    def send_far():
        for key in range(planes - 1, planes // 2 - 1, -1):
            send_queries(key)

    def slot(kind, i, k):
        g = (mine + KEY_VALUE_HEADS - i) % KEY_VALUE_HEADS
        return sources[kind][1].at[:, g, flip(rank, k, share)]

    def passing(kind, i, number, k):
        step = 1 if number == final else steps[number]
        return remote(
            slot(kind, i, k),
            slot(kind, i, k),
            s.fw_send.at[kind, i, number, k // 2],
            s.fw_recv.at[kind, i, k + step],
            mate if number == final else mine * share + flip(rank, step, share),
        )

    def pass_on(kind, chosen):
        known = [0]
        for number, step in enumerate(steps):
            for i in chosen:
                if number == 0:
                    if i > 0:
                        landed(slot(kind, i, 0), s.kv_recv.at[kind, i])
                    else:
                        local[kind].wait()
                for k in known:
                    passing(kind, i, number, k).start()
                if number == 0:
                    passing(kind, i, final, 0).start()
            for i in chosen:
                for k in known:
                    landed(slot(kind, i, k + step), s.fw_recv.at[kind, i, k + step])
                    passing(kind, i, final, k + step).start()
            known = known + [k + step for k in known]

    def pass_end(kind, chosen):
        for i in chosen:
            for k in range(0, share, 2):
                landed(slot(kind, i, k + 1), s.fw_recv.at[kind, i, k + 1])

    pass_on(0, groups)
    pl.when(outer)(send_far)
    pass_on(1, groups)
    pass_end(0, groups)
    pass_end(1, groups[:1])
    landed(s.proj_mate, s.mate_recv.at[m])
    weights[0].wait()

    key_count = s.kv.shape[3]
    scale = HEAD_SIZE ** (-0.5)

    def target(t):
        turn, above = t - 1, planes - 1 - z
        rising = jnp.where(turn < above, planes - 1 - turn, turn - above)
        falling = jnp.where(turn < z, turn, planes - 1 - (turn - z))
        return jnp.where(t == 0, z, jnp.where(z < planes // 2, rising, falling))

    def attend(t):
        @pl.loop(0, 2)
        def _(line):
            c = target(t) * 2 + (y + 1 + line) % 2
            for cc in range(2):
                landed(s.q.at[2 * c + cc], s.q_recv.at[2 * c + cc])
            keys = s.kv[0].reshape(n * key_count, HEAD_SIZE)
            values = s.kv[1].reshape(n * key_count, HEAD_SIZE)
            fresh_key = s.own[0, (2 * c) // share, pl.ds((2 * c) % share, 2)]
            fresh_key = fresh_key.reshape(2 * rows, HEAD_SIZE).astype(jnp.float32)
            fresh_value = s.own[1, (2 * c) // share, pl.ds((2 * c) % share, 2)]
            fresh_value = fresh_value.reshape(2 * rows, HEAD_SIZE).astype(jnp.float32)
            for h in range(per):
                lanes = slice(h * HEAD_SIZE, (h + 1) * HEAD_SIZE)
                q = s.q[pl.ds(2 * c, 2), :, lanes].reshape(2 * rows, HEAD_SIZE)
                scores = lax.dot_general(
                    q, keys, (((1,), (1,)), ((), ())), preferred_element_type=jnp.float32
                )
                own = jnp.sum(q.astype(jnp.float32) * fresh_key, axis=-1, keepdims=True)
                peak = jnp.maximum(own, jnp.max(scores, axis=-1, keepdims=True))
                weight = jnp.exp((scores - peak) * scale)
                own = jnp.exp((own - peak) * scale)
                total = jnp.sum(weight, axis=-1, keepdims=True) + own
                mixed = jnp.dot(
                    weight.astype(jnp.bfloat16), values, preferred_element_type=jnp.float32
                )
                mixed = (mixed + own * fresh_value) / total
                s.att[c, :, :, lanes] = mixed.astype(jnp.bfloat16).reshape(2, rows, HEAD_SIZE)
            remote(
                s.att.at[c, 1 - core],
                s.att_mate.at[c],
                s.mate_send.at[c],
                s.mate_recv.at[c],
                mate,
            ).start()

    def project(t):
        zd = target(t)
        chips = [zd * 2 + (1 - y), zd * 2 + y]
        for c in chips:
            landed(s.att_mate.at[c], s.mate_recv.at[c])
        left = jnp.concatenate([s.att[c, core] for c in chips], axis=0)
        left_mate = jnp.concatenate([s.att_mate[c] for c in chips], axis=0)
        for half in range(2):

            for i in range(half_width // COLUMNS_STEP):
                part = pl.ds(i * COLUMNS_STEP, COLUMNS_STEP)
                at = pl.ds(half * half_width + i * COLUMNS_STEP, COLUMNS_STEP)
                product = jnp.dot(
                    left, s.proj_mine[:, at], preferred_element_type=jnp.float32
                ) + jnp.dot(left_mate, s.proj_mate[:, at], preferred_element_type=jnp.float32)
                s.outgoing[0, zd, half, :, part] = product[:rows].astype(jnp.bfloat16)
                s.outgoing[1, zd, half, :, part] = product[rows:].astype(jnp.bfloat16)

            remote(
                s.outgoing.at[0, zd, half],
                s.y_in.at[zd, half],
                s.y_send.at[zd, half],
                s.y_recv.at[zd, half],
                across,
            ).start()

    def from_line(zd, way, half):
        landed(s.incoming.at[way, zd, half], s.z_recv.at[way, zd, half])

    def relay(t):
        zd = target(t)
        way = jnp.where(zd > z, RIGHT, LEFT)
        inner = jnp.where(zd > z, z > 0, z < planes - 1)
        other = device(jnp.where(zd > z, z + 1, z - 1), y, core)
        for half in range(2):
            landed(s.y_in.at[zd, half], s.y_recv.at[zd, half])

            @pl.when(inner)
            def _():
                from_line(zd, way, half)
                total = (
                    s.outgoing[1, zd, half].astype(jnp.float32)
                    + s.y_in[zd, half].astype(jnp.float32)
                    + s.incoming[way, zd, half].astype(jnp.float32)
                )
                s.outgoing[1, zd, half] = total.astype(jnp.bfloat16)

            @pl.when(jnp.logical_not(inner))
            def _():
                total = s.outgoing[1, zd, half].astype(jnp.float32) + s.y_in[zd, half].astype(
                    jnp.float32
                )
                s.outgoing[1, zd, half] = total.astype(jnp.bfloat16)

            remote(
                s.outgoing.at[1, zd, half],
                s.incoming.at[way, zd, half],
                s.z_send.at[zd, half],
                s.z_recv.at[way, zd, half],
                other,
            ).start()

    pl.when(jnp.logical_not(outer))(send_far)

    @pl.loop(0, planes + 2)
    def _(u):
        @pl.when(u == 1)
        def _():
            fill_tables()
            pass_end(1, groups[1:])

        @pl.when(u < planes)
        def _():
            attend(u)

        @pl.when(u == 0)
        def _():
            for key in range(planes // 2 - 1, 0, -1):
                send_queries(key)

        @pl.when(u < planes)
        def _():
            project(u)

        early = jnp.logical_and(outer, jnp.logical_and(u > 1, u <= planes))

        @pl.when(early)
        def _():
            relay(u - 1)

        @pl.when(jnp.logical_and(jnp.logical_not(outer), u > 2))
        def _():
            relay(u - 2)

    squares = 0.0
    for half in range(2):
        landed(s.y_in.at[z, half], s.y_recv.at[z, half])
        s.part[half] = (
            s.outgoing[1, z, half].astype(jnp.float32)
            + s.y_in[z, half].astype(jnp.float32)
            + residual[:, cols[half]].astype(jnp.float32)
        )
        for way, there in ((RIGHT, z > 0), (LEFT, z < planes - 1)):

            @pl.when(there)
            def _():
                from_line(z, way, half)
                s.part[half] = s.part[half] + s.incoming[way, z, half].astype(jnp.float32)

        value = s.part[half].astype(jnp.bfloat16)
        hidden[:, cols[half]] = value
        value = value.astype(jnp.float32)
        squares = squares + jnp.sum(value * value, axis=-1, keepdims=True)
    factor = lax.rsqrt(squares / width + epsilon)
    for half in range(2):
        value = hidden[:, cols[half]].astype(jnp.float32)
        s.normed[:, cols[half]] = (value * factor * gain[:, cols[half]]).astype(jnp.bfloat16)

    p = place_of(chip, m)

    def at(offset, c):
        return chip_at((p + offset + m) % m, m) * 2 + c

    neighbour = (at(1, core), at(-1, core))
    offsets = [0]
    for d in range(1, reach):
        offsets += [-d, d]
    offsets.append(reach)

    def forward(src, owner, way, half, d):
        send(
            src,
            s.held.at[owner, :, cols[half]],
            s.ring_send.at[way, d, half],
            s.ring_recv.at[way, d, half],
            neighbour[way],
        )

    for way, half in PAIRS:
        forward(s.normed.at[:, cols[half]], me, way, half, 0)
    send(s.normed, s.held.at[me], s.pass_send.at[0, 0, 0], s.pass_recv.at[0, 0, 0], mate)
    s.held[me] = s.normed[...]
    for key in range(planes):
        zd = flip(z, key, planes)
        for half in range(2):
            remote(
                s.outgoing.at[0, zd, half],
                s.y_in.at[zd, half],
                s.y_send.at[zd, half],
                s.y_recv.at[zd, half],
                across,
            ).wait_send()
            if key > 0:
                remote(
                    s.outgoing.at[1, zd, half],
                    s.incoming.at[0, zd, half],
                    s.z_send.at[zd, half],
                    s.z_recv.at[0, zd, half],
                    across,
                ).wait_send()
    for c in range(m):
        remote(
            s.att.at[c, 1 - core], s.att_mate.at[c], s.mate_send.at[c], s.mate_recv.at[c], mate
        ).wait_send()
    for key in range(planes):
        send_queries(key, start=False)
    for kind in range(2):
        for i in groups:
            known = [0]
            for number, step in enumerate(steps):
                for k in known:
                    passing(kind, i, number, k).wait_send()
                known = known + [k + step for k in known]
            for k in known:
                passing(kind, i, final, k).wait_send()
    for j in range(1, n):
        table_copy(j).wait_send()
        landed(s.tables.at[(me + n - j) % n], s.t_recv.at[j])

    def wait_mate(offset):
        if offset == 0:
            landed(s.held.at[mate], s.pass_recv.at[0, 0, 0])
            return
        d = abs(offset)
        for way, half in PAIRS:
            if travels(way, half, d, reach) and (d == reach or (way == RIGHT) == (offset < 0)):
                landed(
                    s.held.at[at(offset, 1 - core), :, cols[half]], s.pass_recv.at[way, d, half]
                )

    spots = lax.broadcasted_iota(jnp.int32, (places, LANES), 0).astype(jnp.float32)

    def pick(offset):
        k = offsets.index(offset)
        wait_mate(offset)
        for cc in range(2):
            owner = at(offset, cc)
            marks = []
            for e in range(local_count):
                place = s.tables[owner, pl.ds(core * local_count + e, 1), :]
                marks.append(jnp.where(spots == place, 1.0, 0.0))
            marks = jnp.concatenate(marks, axis=0)[:, :rows].astype(jnp.bfloat16)

            for i in range(width // COLUMNS_STEP):
                part = pl.ds(i * COLUMNS_STEP, COLUMNS_STEP)
                picked = jnp.dot(
                    marks, s.held[owner, :, part], preferred_element_type=jnp.float32
                ).astype(jnp.bfloat16)
                for e in range(local_count):
                    s.rows_in[2 * k + cc, e, :, part] = picked[e * places : (e + 1) * places]

        owner = at(offset, core)
        shares = []
        for side in (core, 1 - core):
            for e in range(local_count):
                place = s.tables[owner, pl.ds(side * local_count + e, 1), :]
                portion = s.tables[owner, pl.ds((2 + side) * local_count + e, 1), :]
                shares.append(jnp.where(spots == place, portion, 0.0))
        shares = jnp.concatenate(shares, axis=0).T
        s.mix[k] = shares[:rows].astype(jnp.bfloat16)

    def expand(e, f, first, last):
        count = (last - first) * places
        x = s.rows_in[first:last, e].reshape(count, width)
        gate = jnp.dot(
            x, s.gate_up[e, :, f * FF_STEP : (f + 1) * FF_STEP], preferred_element_type=jnp.float32
        )
        up = jnp.dot(
            x,
            s.gate_up[e, :, ff + f * FF_STEP : ff + (f + 1) * FF_STEP],
            preferred_element_type=jnp.float32,
        )
        value = gate / (1.0 + jnp.exp(-gate)) * up
        s.active[e, first * places : last * places, f * FF_STEP : (f + 1) * FF_STEP] = value.astype(
            jnp.bfloat16
        )

    def contract(e, first, last):
        count = (last - first) * places

        for i in range(width // COLUMNS_STEP):
            part = pl.ds(i * COLUMNS_STEP, COLUMNS_STEP)
            value = jnp.dot(
                s.active[e, first * places : last * places, :],
                s.down[e, :, part],
                preferred_element_type=jnp.float32,
            )
            s.rows_in[first:last, e, :, part] = value.astype(jnp.bfloat16).reshape(
                last - first, places, COLUMNS_STEP
            )

    def trade(first, last):
        for k in reversed(range(first // 2, last // 2)):
            send(
                s.rows_in.at[2 * k + 1 - core],
                s.rows_mate.at[k],
                s.trade_send.at[k],
                s.trade_recv.at[k],
                mate,
            )

    def expert_jobs(first, last):
        jobs = []
        for e in range(local_count):
            for f in range(ff // FF_STEP):
                jobs.append(functools.partial(expand, e, f, first, last))
        for e in range(local_count):
            jobs.append(functools.partial(contract, e, first, last))
        jobs.append(functools.partial(trade, first, last))
        return jobs

    early, later = 2 * (2 * reach - 5), 2 * (2 * reach - 3)
    jobs = deque()
    waits = {d: sum(travels(way, half, d, reach) for way, half in PAIRS) for d in range(1, reach + 1)}
    left = sum(waits.values())

    def level(d):
        found = [o for o in offsets if abs(o) == d]
        return [functools.partial(pick, o) for o in found]

    for d in range(1, reach + 1):
        jobs.extend(level(d - 1))
        if d == reach - 2:
            for copy in weights[1:]:
                jobs.append(copy.wait)
            jobs.extend(expert_jobs(0, early))
        if d == reach - 1:
            jobs.extend(expert_jobs(early, later))
        for way, half in PAIRS:
            if not travels(way, half, d, reach):
                continue
            owner = at(-d if way == RIGHT else d, core)
            piece = s.held.at[owner, :, cols[half]]
            landed(piece, s.ring_recv.at[way, d - 1, half])
            if travels(way, half, d + 1, reach):
                forward(piece, owner, way, half, d)
            send(piece, piece, s.pass_send.at[way, d, half], s.pass_recv.at[way, d, half], mate)
            for _ in range(-(-len(jobs) // left)):
                jobs.popleft()()
            left -= 1
    jobs.extend(level(reach))
    while jobs:
        jobs.popleft()()
    for job in expert_jobs(later, 2 * m):
        job()

    traded = set()

    def portion(offset, half, i):
        k = offsets.index(offset)
        part = pl.ds(half * half_width + i * COLUMNS_STEP, COLUMNS_STEP)
        depth = local_count * places
        both = jnp.concatenate(
            [
                s.rows_in[2 * k + core, :, :, part].reshape(depth, COLUMNS_STEP),
                s.rows_mate[k, :, :, part].reshape(depth, COLUMNS_STEP),
            ],
            axis=0,
        )
        return jnp.dot(s.mix[k], both, preferred_element_type=jnp.float32)

    def meet(offset):
        k = offsets.index(offset)
        if k not in traded:
            landed(s.rows_mate.at[k], s.trade_recv.at[k])
            traded.add(k)

    for d in range(reach, 0, -1):
        for way, half in ((RIGHT, 1), (LEFT, 0), (RIGHT, 0), (LEFT, 1)):
            if not travels(way, half, d, reach):
                continue
            offset = d if (way == RIGHT or d == reach) else -d
            meet(offset)
            adds = travels(way, half, d + 1, reach)
            if adds:
                landed(s.incoming.at[way, d, half], s.back_recv.at[way, d, half])

            for i in range(half_width // COLUMNS_STEP):
                part = pl.ds(i * COLUMNS_STEP, COLUMNS_STEP)
                total = portion(offset, half, i)
                if adds:
                    total = total + s.incoming[way, d, half, :, part].astype(jnp.float32)
                s.outgoing[way, d - 1, half, :, part] = total.astype(jnp.bfloat16)

            send(
                s.outgoing.at[way, d - 1, half],
                s.incoming.at[way, d - 1, half],
                s.back_send.at[way, d - 1, half],
                s.back_recv.at[way, d - 1, half],
                neighbour[way],
            )
    meet(0)
    for half in range(2):
        for way in (RIGHT, LEFT):
            landed(s.incoming.at[way, 0, half], s.back_recv.at[way, 0, half])

        for i in range(half_width // COLUMNS_STEP):
            part = pl.ds(i * COLUMNS_STEP, COLUMNS_STEP)
            out = pl.ds(half * half_width + i * COLUMNS_STEP, COLUMNS_STEP)
            total = portion(0, half, i)
            for way in (RIGHT, LEFT):
                total = total + s.incoming[way, 0, half, :, part].astype(jnp.float32)
            result[:, out] = total.astype(jnp.bfloat16)

    finish_sends()


def keep_kernel(hidden, result, hidden_out, result_out):
    hidden_out[...] = hidden[...]
    result_out[...] = result[...]


def local(
    n,
    queries,
    fresh_key_value,
    cache_key_value,
    residual,
    norm_gain,
    out_proj,
    w_gate_up,
    w_down,
    route_ids,
    route_weights,
    placement,
):
    rows, width = residual.shape
    experts = placement.shape[0]
    local_count, _, wide = w_gate_up.shape
    key_count = cache_key_value.shape[1]
    places = block_places(rows, experts)
    m, planes, reach = n // 2, n // 4, n // 4
    share = n // KEY_VALUE_HEADS
    head_width = QUERY_HEADS // n * HEAD_SIZE
    levels = max(1, share.bit_length() - 2)
    half = width // 2
    narrow = jnp.bfloat16
    sems = pltpu.SemaphoreType.DMA
    scratch = dict(
        kv=pltpu.VMEM((2, KEY_VALUE_HEADS, share, key_count, HEAD_SIZE), narrow),
        own=pltpu.VMEM((2, KEY_VALUE_HEADS, share, rows, HEAD_SIZE), narrow),
        q=pltpu.VMEM((n, rows, head_width), narrow),
        proj_mine=pltpu.VMEM((head_width, width), narrow),
        proj_mate=pltpu.VMEM((head_width, width), narrow),
        gate_up=pltpu.VMEM(w_gate_up.shape, narrow),
        down=pltpu.VMEM(w_down.shape, narrow),
        table=pltpu.VMEM((m, 4 * local_count, LANES), jnp.float32),
        tables=pltpu.VMEM((n, 4 * local_count, LANES), jnp.float32),
        att=pltpu.VMEM((m, 2, rows, head_width), narrow),
        att_mate=pltpu.VMEM((m, rows, head_width), narrow),
        part=pltpu.VMEM((2, rows, half), jnp.float32),
        y_in=pltpu.VMEM((planes, 2, rows, half), narrow),
        outgoing=pltpu.VMEM((2, reach, 2, rows, half), narrow),
        incoming=pltpu.VMEM((2, reach, 2, rows, half), narrow),
        normed=pltpu.VMEM((rows, width), narrow),
        held=pltpu.VMEM((n, rows, width), narrow),
        rows_in=pltpu.VMEM((n, local_count, places, width), narrow),
        rows_mate=pltpu.VMEM((m, local_count, places, width), narrow),
        active=pltpu.VMEM((local_count, n * places, wide // 2), narrow),
        mix=pltpu.VMEM((m, rows, 2 * local_count * places), narrow),
        kv_send=sems((2, KEY_VALUE_HEADS)),
        kv_recv=sems((2, KEY_VALUE_HEADS)),
        fw_send=sems((2, KEY_VALUE_HEADS, levels + 1, share // 2)),
        fw_recv=sems((2, KEY_VALUE_HEADS, share)),
        q_send=sems((n,)),
        q_recv=sems((n,)),
        t_send=sems((n,)),
        t_recv=sems((n,)),
        load=sems((3,)),
        mate_send=sems((m + 1,)),
        mate_recv=sems((m + 1,)),
        y_send=sems((planes, 2)),
        y_recv=sems((planes, 2)),
        z_send=sems((planes, 2)),
        z_recv=sems((2, planes, 2)),
        ring_send=sems((2, reach, 2)),
        ring_recv=sems((2, reach, 2)),
        pass_send=sems((2, reach + 1, 2)),
        pass_recv=sems((2, reach + 1, 2)),
        trade_send=sems((m,)),
        trade_recv=sems((m,)),
        back_send=sems((2, reach, 2)),
        back_recv=sems((2, reach, 2)),
    )
    hidden, result = pl.pallas_call(
        functools.partial(whole_kernel, n, tuple(scratch)),
        out_shape=[jax.ShapeDtypeStruct((rows, width), narrow)] * 2,
        in_specs=[ANY] * 6 + [VMEM] * 5,
        out_specs=[VMEM] * 2,
        scratch_shapes=list(scratch.values()),
        compiler_params=pltpu.CompilerParams(
            collective_id=0, has_side_effects=True, vmem_limit_bytes=60 * 2**20
        ),
        name="whole",
    )(
        queries,
        fresh_key_value,
        cache_key_value,
        out_proj,
        w_gate_up,
        w_down,
        residual,
        norm_gain.reshape(1, -1),
        route_ids.T,
        route_weights.T,
        placement.reshape(1, -1),
    )
    return pl.pallas_call(
        keep_kernel,
        out_shape=[jax.ShapeDtypeStruct((rows, width), narrow)] * 2,
        in_specs=[VMEM] * 2,
        out_specs=[VMEM] * 2,
        name="keep",
    )(hidden, result)


def solution(mesh):
    in_specs = (
        P(("groups", "ctx"), None),
        P(None, ("groups", "ctx"), None),
        P(None, ("groups", "ctx"), None),
        P(("groups", "ctx"), None),
        P(),
        P("ctx", None),
        P("ctx", None, None),
        P("ctx", None, None),
        P(("groups", "ctx"), None),
        P(("groups", "ctx"), None),
        P(),
    )
    out_specs = (P(("groups", "ctx"), None), P(("groups", "ctx"), None))
    return jax.shard_map(
        functools.partial(local, mesh.shape["ctx"]),
        mesh=mesh,
        in_specs=in_specs,
        out_specs=out_specs,
        check_vma=False,
    )
```

```python
import functools
import types
from collections import deque

import jax
import jax.numpy as jnp
from jax import lax
from jax.experimental import pallas as pl
from jax.experimental.pallas import tpu as pltpu
from jax.sharding import PartitionSpec as P

QUERY_HEADS = 32
KEY_VALUE_HEADS = 4
HEAD_SIZE = 128
TOPK = 8
COLUMNS_STEP = 1024
FF_STEP = 256
LANES = 128

epsilon = 1e-06

VMEM = pl.BlockSpec(memory_space=pltpu.VMEM)
ANY = pl.BlockSpec(memory_space=pl.ANY)
RIGHT, LEFT = 0, 1
PAIRS = ((RIGHT, 0), (LEFT, 1), (RIGHT, 1), (LEFT, 0))


def chip_at(q, m):
    return jnp.where(q < m // 2, 2 * q, 2 * (m - 1 - q) + 1)


def place_of(chip, m):
    return jnp.where(chip % 2 == 0, chip // 2, m - 1 - chip // 2)


def flip(value, key, size):
    total, bit = 0, 1
    while bit < size:
        total = total + (value // bit + key // bit) % 2 * bit
        bit *= 2
    return total


def greet(others):
    barrier = pltpu.get_barrier_semaphore()
    for other in others:
        pl.semaphore_signal(
            barrier, inc=1, device_id={"ctx": other}, device_id_type=pl.DeviceIdType.MESH
        )
    pl.semaphore_wait(barrier, len(others))


def remote(src, dst, send, recv, other):
    return pltpu.make_async_remote_copy(
        src_ref=src,
        dst_ref=dst,
        send_sem=send,
        recv_sem=recv,
        device_id={"ctx": other},
        device_id_type=pl.DeviceIdType.MESH,
    )


def landed(piece, sem):
    pltpu.make_async_copy(piece, piece, sem).wait()


def travels(way, half, d, reach):
    return d < reach or (d == reach and half == way)


def block_places(rows, experts):
    most = max(2, 3 * rows * TOPK // (2 * experts))
    return -(-most // 16) * 16


def whole_kernel(
    n,
    names,
    queries,
    fresh,
    cache,
    proj,
    gate_up,
    down,
    residual,
    gain,
    ids,
    route,
    placement,
    hidden,
    result,
    *scratch,
):
    s = types.SimpleNamespace(**dict(zip(names, scratch)))
    m, planes, reach = n // 2, n // 4, n // 4
    rows, width = residual.shape
    half_width = width // 2
    cols = [pl.ds(h * half_width, half_width) for h in range(2)]
    local_count, _, wide = gate_up.shape
    ff = wide // 2
    experts = placement.shape[1]
    places = s.rows_in.shape[2]
    per = QUERY_HEADS // n
    head_width = per * HEAD_SIZE
    share = n // KEY_VALUE_HEADS

    me = lax.axis_index("ctx")
    core, chip = me % 2, me // 2
    y, z = chip % 2, chip // 2

    def device(zz, yy, cc):
        return (zz * 2 + yy) * 2 + cc

    mate = device(z, y, 1 - core)
    across = device(z, 1 - y, core)
    started = []

    def send(src, dst, send_sem, recv_sem, other):
        copy = remote(src, dst, send_sem, recv_sem, other)
        copy.start()
        started.append(copy)

    def finish_sends():
        while started:
            started.pop(0).wait_send()

    greet([(me + j) % n for j in range(1, n)])

    mine, rank = me // share, me % share
    sources = ((cache, s.kv), (fresh, s.own))

    def lanes_of(head):
        return pl.ds(pl.multiple_of(head * HEAD_SIZE, HEAD_SIZE), HEAD_SIZE)

    local = []
    for kind, (src, dst) in enumerate(sources):
        copy = pltpu.make_async_copy(
            src.at[:, :, lanes_of(mine)], dst.at[:, mine, rank], s.kv_recv.at[kind, 0]
        )
        copy.start()
        local.append(copy)

    def spread_kv(kind):
        src, dst = sources[kind]
        for i in range(1, KEY_VALUE_HEADS):
            head = (mine + i) % KEY_VALUE_HEADS
            send(
                src.at[:, :, lanes_of(head)],
                dst.at[:, mine, rank],
                s.kv_send.at[kind, i],
                s.kv_recv.at[kind, i],
                head * share + rank,
            )

    spread_kv(0)
    spread_kv(1)

    copy = pltpu.make_async_copy(
        queries.at[:, pl.ds(pl.multiple_of(me * head_width, LANES), head_width)],
        s.q.at[me],
        s.q_recv.at[me],
    )
    copy.start()

    def send_queries(key, start=True):
        for dy in (1, 0):
            for dc in (0, 1):
                if (key, dy, dc) == (0, 0, 0):
                    continue
                other = device(flip(z, key, planes), (y + dy) % 2, (core + dc) % 2)
                copy = remote(
                    queries.at[:, pl.ds(pl.multiple_of(other * head_width, LANES), head_width)],
                    s.q.at[me],
                    s.q_send.at[key * 4 + dy * 2 + dc],
                    s.q_recv.at[me],
                    other,
                )
                if start:
                    copy.start()
                else:
                    copy.wait_send()

    for key in range(planes // 2 - 1, -1, -1):
        send_queries(key)
    send(proj, s.proj_mate, s.mate_send.at[m], s.mate_recv.at[m], mate)
    weights = [
        pltpu.make_async_copy(proj, s.proj_mine, s.load.at[0]),
        pltpu.make_async_copy(gate_up, s.gate_up, s.load.at[1]),
        pltpu.make_async_copy(down, s.down, s.load.at[2]),
    ]
    for copy in weights:
        copy.start()

    def table_copy(j):
        other = (me + j) % n
        return remote(
            s.table.at[other // 2], s.tables.at[me], s.t_send.at[j], s.t_recv.at[j], other
        )

    def fill_tables():
        scores = route[...]
        scores = scores / jnp.sum(scores, axis=0, keepdims=True)
        listed = lax.broadcasted_iota(jnp.int32, (experts, rows), 0)
        by_expert = jnp.zeros((experts, rows), jnp.float32)
        for k in range(TOPK):
            by_expert = by_expert + jnp.where(listed == ids[k : k + 1], scores[k : k + 1], 0.0)
        by_expert = jnp.concatenate(
            [by_expert, jnp.zeros((experts, LANES - rows), jnp.float32)], axis=1
        ).astype(jnp.bfloat16)
        moved = jnp.where(
            lax.broadcasted_iota(jnp.int32, (experts, experts), 0) == placement[...], 1.0, 0.0
        ).astype(jnp.bfloat16)
        by_slot = jnp.dot(moved, by_expert, preferred_element_type=jnp.float32)
        named = jnp.where(by_slot > 0, 1.0, 0.0)
        before = jnp.where(
            lax.broadcasted_iota(jnp.int32, (LANES, LANES), 0)
            < lax.broadcasted_iota(jnp.int32, (LANES, LANES), 1),
            1.0,
            0.0,
        ).astype(jnp.bfloat16)
        ranks = jnp.dot(named.astype(jnp.bfloat16), before, preferred_element_type=jnp.float32)
        ranks = jnp.where(by_slot > 0, ranks, -1.0)
        pair = 2 * local_count
        for c in range(m):
            s.table[c, 0:pair, :] = ranks[c * pair : (c + 1) * pair]
            s.table[c, pair : 2 * pair, :] = by_slot[c * pair : (c + 1) * pair]
        s.tables[me] = s.table[chip]
        for j in range(1, n):
            table_copy(j).start()

    steps = []
    bit = 2
    while bit < share:
        steps.append(bit)
        bit *= 2
    final = len(steps)
    groups = tuple(range(KEY_VALUE_HEADS))
    outer = jnp.logical_or(z < planes // 4, z >= planes - planes // 4)

    def send_far():
        for key in range(planes - 1, planes // 2 - 1, -1):
            send_queries(key)

    def slot(kind, i, k):
        g = (mine + KEY_VALUE_HEADS - i) % KEY_VALUE_HEADS
        return sources[kind][1].at[:, g, flip(rank, k, share)]

    def passing(kind, i, number, k):
        step = 1 if number == final else steps[number]
        return remote(
            slot(kind, i, k),
            slot(kind, i, k),
            s.fw_send.at[kind, i, number, k // 2],
            s.fw_recv.at[kind, i, k + step],
            mate if number == final else mine * share + flip(rank, step, share),
        )

    def pass_on(kind, chosen):
        known = [0]
        for number, step in enumerate(steps):
            for i in chosen:
                if number == 0:
                    if i > 0:
                        landed(slot(kind, i, 0), s.kv_recv.at[kind, i])
                    else:
                        local[kind].wait()
                for k in known:
                    passing(kind, i, number, k).start()
                if number == 0:
                    passing(kind, i, final, 0).start()
            for i in chosen:
                for k in known:
                    landed(slot(kind, i, k + step), s.fw_recv.at[kind, i, k + step])
                    passing(kind, i, final, k + step).start()
            known = known + [k + step for k in known]

    def pass_end(kind, chosen):
        for i in chosen:
            for k in range(0, share, 2):
                landed(slot(kind, i, k + 1), s.fw_recv.at[kind, i, k + 1])

    pass_on(0, groups)
    send_far()
    pass_on(1, groups)
    pass_end(0, groups)
    pass_end(1, groups)
    landed(s.proj_mate, s.mate_recv.at[m])
    weights[0].wait()

    key_count = s.kv.shape[3]
    scale = HEAD_SIZE ** (-0.5)

    near = flip(z, 1, planes)

    def target(t):
        turn, above, lower = t - 1, planes - 1 - z, z < planes // 2
        skipped = jnp.where(
            lower,
            jnp.where(z % 2 == 0, above - 1, planes - 2),
            jnp.where(z % 2 == 1, z - 1, planes - 2),
        )
        turn = turn + jnp.where(turn >= skipped, 1, 0)
        rising = jnp.where(turn < above, planes - 1 - turn, turn - above)
        falling = jnp.where(turn < z, turn, planes - 1 - (turn - z))
        beyond = jnp.where(lower, rising, falling)
        return jnp.where(t == 0, near, jnp.where(t == planes - 1, z, beyond))

    def attend(t):
        @pl.loop(0, 2)
        def _(line):
            c = target(t) * 2 + (y + 1 + line) % 2
            for cc in range(2):
                landed(s.q.at[2 * c + cc], s.q_recv.at[2 * c + cc])
            keys = s.kv[0].reshape(n * key_count, HEAD_SIZE)
            values = s.kv[1].reshape(n * key_count, HEAD_SIZE)
            fresh_key = s.own[0, (2 * c) // share, pl.ds((2 * c) % share, 2)]
            fresh_key = fresh_key.reshape(2 * rows, HEAD_SIZE).astype(jnp.float32)
            fresh_value = s.own[1, (2 * c) // share, pl.ds((2 * c) % share, 2)]
            fresh_value = fresh_value.reshape(2 * rows, HEAD_SIZE).astype(jnp.float32)
            for h in range(per):
                lanes = slice(h * HEAD_SIZE, (h + 1) * HEAD_SIZE)
                q = s.q[pl.ds(2 * c, 2), :, lanes].reshape(2 * rows, HEAD_SIZE)
                scores = lax.dot_general(
                    q, keys, (((1,), (1,)), ((), ())), preferred_element_type=jnp.float32
                )
                own = jnp.sum(q.astype(jnp.float32) * fresh_key, axis=-1, keepdims=True)
                peak = jnp.maximum(own, jnp.max(scores, axis=-1, keepdims=True))
                weight = jnp.exp((scores - peak) * scale)
                own = jnp.exp((own - peak) * scale)
                total = jnp.sum(weight, axis=-1, keepdims=True) + own
                mixed = jnp.dot(
                    weight.astype(jnp.bfloat16), values, preferred_element_type=jnp.float32
                )
                mixed = (mixed + own * fresh_value) / total
                s.att[c, :, :, lanes] = mixed.astype(jnp.bfloat16).reshape(2, rows, HEAD_SIZE)
            remote(
                s.att.at[c, 1 - core],
                s.att_mate.at[c],
                s.mate_send.at[c],
                s.mate_recv.at[c],
                mate,
            ).start()

    def project(t):
        zd = target(t)
        chips = [zd * 2 + (1 - y), zd * 2 + y]
        for c in chips:
            landed(s.att_mate.at[c], s.mate_recv.at[c])
        left = jnp.concatenate([s.att[c, core] for c in chips], axis=0)
        left_mate = jnp.concatenate([s.att_mate[c] for c in chips], axis=0)
        for half in range(2):

            for i in range(half_width // COLUMNS_STEP):
                part = pl.ds(i * COLUMNS_STEP, COLUMNS_STEP)
                at = pl.ds(half * half_width + i * COLUMNS_STEP, COLUMNS_STEP)
                product = jnp.dot(
                    left, s.proj_mine[:, at], preferred_element_type=jnp.float32
                ) + jnp.dot(left_mate, s.proj_mate[:, at], preferred_element_type=jnp.float32)
                if half == 0:
                    s.outgoing[0, zd, half, :, part] = product[:rows].astype(jnp.bfloat16)
                else:

                    @pl.when(t < planes - 1)
                    def _():
                        s.outgoing[0, zd, half, :, part] = product[:rows].astype(jnp.bfloat16)

                    @pl.when(t == planes - 1)
                    def _():
                        if i == 0:
                            landed(s.turned, s.turn_recv.at[0])
                        total = product[:rows] + s.turned[:, part].astype(jnp.float32)
                        s.outgoing[0, zd, half, :, part] = total.astype(jnp.bfloat16)

                s.outgoing[1, zd, half, :, part] = product[rows:].astype(jnp.bfloat16)

            def go_across(half=half):
                remote(
                    s.outgoing.at[0, zd, half],
                    s.y_in.at[zd, half],
                    s.y_send.at[zd, half],
                    s.y_recv.at[zd, half],
                    across,
                ).start()

            if half == 0:
                go_across()
            else:
                pl.when(t > 0)(go_across)

                @pl.when(t == 0)
                def _():
                    remote(
                        s.outgoing.at[0, zd, half],
                        s.turned,
                        s.y_send.at[zd, half],
                        s.turn_recv.at[0],
                        device(near, y, core),
                    ).start()


    def from_line(zd, way, half):
        landed(s.incoming.at[way, zd, half], s.z_recv.at[way, zd, half])

    def relay(t):
        zd = target(t)
        way = jnp.where(zd > z, RIGHT, LEFT)
        inner = jnp.where(zd > z, z > 0, z < planes - 1)
        other = device(jnp.where(zd > z, z + 1, z - 1), y, core)
        for half in range(2):
            s.part[half] = s.outgoing[1, zd, half].astype(jnp.float32)

            def from_across(half=half):
                landed(s.y_in.at[zd, half], s.y_recv.at[zd, half])
                s.part[half] = s.part[half] + s.y_in[zd, half].astype(jnp.float32)

            if half == 0:
                from_across()
            else:
                pl.when(t > 0)(from_across)

            @pl.when(inner)
            def _():
                from_line(zd, way, half)
                s.part[half] = s.part[half] + s.incoming[way, zd, half].astype(jnp.float32)

            s.outgoing[1, zd, half] = s.part[half].astype(jnp.bfloat16)
            remote(
                s.outgoing.at[1, zd, half],
                s.incoming.at[way, zd, half],
                s.z_send.at[zd, half],
                s.z_recv.at[way, zd, half],
                other,
            ).start()


    @pl.loop(0, planes + 2)
    def _(u):
        @pl.when(u == 1)
        def _():
            fill_tables()

        @pl.when(u < planes)
        def _():
            attend(u)

        @pl.when(u < planes)
        def _():
            project(u)

        early = jnp.logical_and(outer, jnp.logical_and(u > 1, u <= planes))

        @pl.when(early)
        def _():
            relay((u - 1) % (planes - 1))

        @pl.when(jnp.logical_and(jnp.logical_not(outer), u > 2))
        def _():
            relay((u - 2) % (planes - 1))

    squares = 0.0
    for half in range(2):
        landed(s.y_in.at[z, half], s.y_recv.at[z, half])
        s.part[half] = (
            s.outgoing[1, z, half].astype(jnp.float32)
            + s.y_in[z, half].astype(jnp.float32)
            + residual[:, cols[half]].astype(jnp.float32)
        )
        for way, there in ((RIGHT, z > 0), (LEFT, z < planes - 1)):

            @pl.when(there)
            def _():
                from_line(z, way, half)
                s.part[half] = s.part[half] + s.incoming[way, z, half].astype(jnp.float32)

        value = s.part[half].astype(jnp.bfloat16)
        hidden[:, cols[half]] = value
        value = value.astype(jnp.float32)
        squares = squares + jnp.sum(value * value, axis=-1, keepdims=True)
    factor = lax.rsqrt(squares / width + epsilon)
    for half in range(2):
        value = hidden[:, cols[half]].astype(jnp.float32)
        s.normed[:, cols[half]] = (value * factor * gain[:, cols[half]]).astype(jnp.bfloat16)

    p = place_of(chip, m)

    def at(offset, c):
        return chip_at((p + offset + m) % m, m) * 2 + c

    neighbour = (at(1, core), at(-1, core))
    offsets = [0]
    for d in range(1, reach):
        offsets += [-d, d]
    offsets.append(reach)

    def forward(src, owner, way, half, d):
        send(
            src,
            s.held.at[owner, :, cols[half]],
            s.ring_send.at[way, d, half],
            s.ring_recv.at[way, d, half],
            neighbour[way],
        )

    for way, half in PAIRS:
        forward(s.normed.at[:, cols[half]], me, way, half, 0)
    send(s.normed, s.held.at[me], s.pass_send.at[0, 0, 0], s.pass_recv.at[0, 0, 0], mate)
    s.held[me] = s.normed[...]
    for key in range(planes):
        zd = flip(z, key, planes)
        for half in range(2):
            remote(
                s.outgoing.at[0, zd, half],
                s.y_in.at[zd, half],
                s.y_send.at[zd, half],
                s.y_recv.at[zd, half],
                across,
            ).wait_send()
            if key > 0:
                remote(
                    s.outgoing.at[1, zd, half],
                    s.incoming.at[0, zd, half],
                    s.z_send.at[zd, half],
                    s.z_recv.at[0, zd, half],
                    across,
                ).wait_send()
    for c in range(m):
        remote(
            s.att.at[c, 1 - core], s.att_mate.at[c], s.mate_send.at[c], s.mate_recv.at[c], mate
        ).wait_send()
    for key in range(planes):
        send_queries(key, start=False)
    for kind in range(2):
        for i in groups:
            known = [0]
            for number, step in enumerate(steps):
                for k in known:
                    passing(kind, i, number, k).wait_send()
                known = known + [k + step for k in known]
            for k in known:
                passing(kind, i, final, k).wait_send()
    for j in range(1, n):
        table_copy(j).wait_send()
        landed(s.tables.at[(me + n - j) % n], s.t_recv.at[j])

    def wait_mate(offset):
        if offset == 0:
            landed(s.held.at[mate], s.pass_recv.at[0, 0, 0])
            return
        d = abs(offset)
        for way, half in PAIRS:
            if travels(way, half, d, reach) and (d == reach or (way == RIGHT) == (offset < 0)):
                landed(
                    s.held.at[at(offset, 1 - core), :, cols[half]], s.pass_recv.at[way, d, half]
                )

    spots = lax.broadcasted_iota(jnp.int32, (places, LANES), 0).astype(jnp.float32)

    def pick(offset):
        k = offsets.index(offset)
        wait_mate(offset)
        for cc in range(2):
            owner = at(offset, cc)
            marks = []
            for e in range(local_count):
                place = s.tables[owner, pl.ds(core * local_count + e, 1), :]
                marks.append(jnp.where(spots == place, 1.0, 0.0))
            marks = jnp.concatenate(marks, axis=0)[:, :rows].astype(jnp.bfloat16)

            for i in range(width // COLUMNS_STEP):
                part = pl.ds(i * COLUMNS_STEP, COLUMNS_STEP)
                picked = jnp.dot(
                    marks, s.held[owner, :, part], preferred_element_type=jnp.float32
                ).astype(jnp.bfloat16)
                for e in range(local_count):
                    s.rows_in[2 * k + cc, e, :, part] = picked[e * places : (e + 1) * places]

        owner = at(offset, core)
        shares = []
        for side in (core, 1 - core):
            for e in range(local_count):
                place = s.tables[owner, pl.ds(side * local_count + e, 1), :]
                portion = s.tables[owner, pl.ds((2 + side) * local_count + e, 1), :]
                shares.append(jnp.where(spots == place, portion, 0.0))
        shares = jnp.concatenate(shares, axis=0).T
        s.mix[k] = shares[:rows].astype(jnp.bfloat16)

    def expand(e, f, first, last):
        count = (last - first) * places
        x = s.rows_in[first:last, e].reshape(count, width)
        gate = jnp.dot(
            x, s.gate_up[e, :, f * FF_STEP : (f + 1) * FF_STEP], preferred_element_type=jnp.float32
        )
        up = jnp.dot(
            x,
            s.gate_up[e, :, ff + f * FF_STEP : ff + (f + 1) * FF_STEP],
            preferred_element_type=jnp.float32,
        )
        value = gate / (1.0 + jnp.exp(-gate)) * up
        s.active[e, first * places : last * places, f * FF_STEP : (f + 1) * FF_STEP] = value.astype(
            jnp.bfloat16
        )

    def contract(e, first, last):
        count = (last - first) * places

        for i in range(width // COLUMNS_STEP):
            part = pl.ds(i * COLUMNS_STEP, COLUMNS_STEP)
            value = jnp.dot(
                s.active[e, first * places : last * places, :],
                s.down[e, :, part],
                preferred_element_type=jnp.float32,
            )
            s.rows_in[first:last, e, :, part] = value.astype(jnp.bfloat16).reshape(
                last - first, places, COLUMNS_STEP
            )

    def trade(first, last):
        for k in reversed(range(first // 2, last // 2)):
            send(
                s.rows_in.at[2 * k + 1 - core],
                s.rows_mate.at[k],
                s.trade_send.at[k],
                s.trade_recv.at[k],
                mate,
            )

    def expert_jobs(first, last):
        jobs = []
        for e in range(local_count):
            for f in range(ff // FF_STEP):
                jobs.append(functools.partial(expand, e, f, first, last))
        for e in range(local_count):
            jobs.append(functools.partial(contract, e, first, last))
        jobs.append(functools.partial(trade, first, last))
        return jobs

    early, later = 2 * (2 * reach - 5), 2 * (2 * reach - 3)
    jobs = deque()
    waits = {d: sum(travels(way, half, d, reach) for way, half in PAIRS) for d in range(1, reach + 1)}
    left = sum(waits.values())

    def level(d):
        found = [o for o in offsets if abs(o) == d]
        return [functools.partial(pick, o) for o in found]

    for d in range(1, reach + 1):
        jobs.extend(level(d - 1))
        if d == reach - 2:
            for copy in weights[1:]:
                jobs.append(copy.wait)
            jobs.extend(expert_jobs(0, early))
        if d == reach - 1:
            jobs.extend(expert_jobs(early, later))
        for way, half in PAIRS:
            if not travels(way, half, d, reach):
                continue
            owner = at(-d if way == RIGHT else d, core)
            piece = s.held.at[owner, :, cols[half]]
            landed(piece, s.ring_recv.at[way, d - 1, half])
            if travels(way, half, d + 1, reach):
                forward(piece, owner, way, half, d)
            send(piece, piece, s.pass_send.at[way, d, half], s.pass_recv.at[way, d, half], mate)
            for _ in range(-(-len(jobs) // max(left - 1, 1))):
                jobs.popleft()()
            left -= 1
    jobs.extend(level(reach))
    while jobs:
        jobs.popleft()()
    for job in expert_jobs(later, 2 * m):
        job()

    traded = set()

    def portion(offset, half, i):
        k = offsets.index(offset)
        part = pl.ds(half * half_width + i * COLUMNS_STEP, COLUMNS_STEP)
        depth = local_count * places
        both = jnp.concatenate(
            [
                s.rows_in[2 * k + core, :, :, part].reshape(depth, COLUMNS_STEP),
                s.rows_mate[k, :, :, part].reshape(depth, COLUMNS_STEP),
            ],
            axis=0,
        )
        return jnp.dot(s.mix[k], both, preferred_element_type=jnp.float32)

    def meet(offset):
        k = offsets.index(offset)
        if k not in traded:
            landed(s.rows_mate.at[k], s.trade_recv.at[k])
            traded.add(k)

    for d in range(reach, 0, -1):
        for way, half in ((RIGHT, 1), (LEFT, 0), (RIGHT, 0), (LEFT, 1)):
            if not travels(way, half, d, reach):
                continue
            offset = d if (way == RIGHT or d == reach) else -d
            meet(offset)
            adds = travels(way, half, d + 1, reach)
            if adds:
                landed(s.incoming.at[way, d, half], s.back_recv.at[way, d, half])

            for i in range(half_width // COLUMNS_STEP):
                part = pl.ds(i * COLUMNS_STEP, COLUMNS_STEP)
                total = portion(offset, half, i)
                if adds:
                    total = total + s.incoming[way, d, half, :, part].astype(jnp.float32)
                s.outgoing[way, d - 1, half, :, part] = total.astype(jnp.bfloat16)

            send(
                s.outgoing.at[way, d - 1, half],
                s.incoming.at[way, d - 1, half],
                s.back_send.at[way, d - 1, half],
                s.back_recv.at[way, d - 1, half],
                neighbour[way],
            )
    meet(0)
    for half in range(2):
        for way in (RIGHT, LEFT):
            landed(s.incoming.at[way, 0, half], s.back_recv.at[way, 0, half])

        for i in range(half_width // COLUMNS_STEP):
            part = pl.ds(i * COLUMNS_STEP, COLUMNS_STEP)
            out = pl.ds(half * half_width + i * COLUMNS_STEP, COLUMNS_STEP)
            total = portion(0, half, i)
            for way in (RIGHT, LEFT):
                total = total + s.incoming[way, 0, half, :, part].astype(jnp.float32)
            result[:, out] = total.astype(jnp.bfloat16)

    finish_sends()


def keep_kernel(hidden, result, hidden_out, result_out):
    hidden_out[...] = hidden[...]
    result_out[...] = result[...]


def local(
    n,
    queries,
    fresh_key_value,
    cache_key_value,
    residual,
    norm_gain,
    out_proj,
    w_gate_up,
    w_down,
    route_ids,
    route_weights,
    placement,
):
    rows, width = residual.shape
    experts = placement.shape[0]
    local_count, _, wide = w_gate_up.shape
    key_count = cache_key_value.shape[1]
    places = block_places(rows, experts)
    m, planes, reach = n // 2, n // 4, n // 4
    share = n // KEY_VALUE_HEADS
    head_width = QUERY_HEADS // n * HEAD_SIZE
    levels = max(1, share.bit_length() - 2)
    half = width // 2
    narrow = jnp.bfloat16
    sems = pltpu.SemaphoreType.DMA
    scratch = dict(
        kv=pltpu.VMEM((2, KEY_VALUE_HEADS, share, key_count, HEAD_SIZE), narrow),
        own=pltpu.VMEM((2, KEY_VALUE_HEADS, share, rows, HEAD_SIZE), narrow),
        q=pltpu.VMEM((n, rows, head_width), narrow),
        proj_mine=pltpu.VMEM((head_width, width), narrow),
        proj_mate=pltpu.VMEM((head_width, width), narrow),
        gate_up=pltpu.VMEM(w_gate_up.shape, narrow),
        down=pltpu.VMEM(w_down.shape, narrow),
        table=pltpu.VMEM((m, 4 * local_count, LANES), jnp.float32),
        tables=pltpu.VMEM((n, 4 * local_count, LANES), jnp.float32),
        att=pltpu.VMEM((m, 2, rows, head_width), narrow),
        att_mate=pltpu.VMEM((m, rows, head_width), narrow),
        part=pltpu.VMEM((2, rows, half), jnp.float32),
        turned=pltpu.VMEM((rows, half), narrow),
        y_in=pltpu.VMEM((planes, 2, rows, half), narrow),
        outgoing=pltpu.VMEM((2, reach, 2, rows, half), narrow),
        incoming=pltpu.VMEM((2, reach, 2, rows, half), narrow),
        normed=pltpu.VMEM((rows, width), narrow),
        held=pltpu.VMEM((n, rows, width), narrow),
        rows_in=pltpu.VMEM((n, local_count, places, width), narrow),
        rows_mate=pltpu.VMEM((m, local_count, places, width), narrow),
        active=pltpu.VMEM((local_count, n * places, wide // 2), narrow),
        mix=pltpu.VMEM((m, rows, 2 * local_count * places), narrow),
        kv_send=sems((2, KEY_VALUE_HEADS)),
        kv_recv=sems((2, KEY_VALUE_HEADS)),
        fw_send=sems((2, KEY_VALUE_HEADS, levels + 1, share // 2)),
        fw_recv=sems((2, KEY_VALUE_HEADS, share)),
        q_send=sems((n,)),
        q_recv=sems((n,)),
        t_send=sems((n,)),
        t_recv=sems((n,)),
        load=sems((3,)),
        mate_send=sems((m + 1,)),
        mate_recv=sems((m + 1,)),
        y_send=sems((planes, 2)),
        y_recv=sems((planes, 2)),
        turn_recv=sems((1,)),
        z_send=sems((planes, 2)),
        z_recv=sems((2, planes, 2)),
        ring_send=sems((2, reach, 2)),
        ring_recv=sems((2, reach, 2)),
        pass_send=sems((2, reach + 1, 2)),
        pass_recv=sems((2, reach + 1, 2)),
        trade_send=sems((m,)),
        trade_recv=sems((m,)),
        back_send=sems((2, reach, 2)),
        back_recv=sems((2, reach, 2)),
    )
    hidden, result = pl.pallas_call(
        functools.partial(whole_kernel, n, tuple(scratch)),
        out_shape=[jax.ShapeDtypeStruct((rows, width), narrow)] * 2,
        in_specs=[ANY] * 6 + [VMEM] * 5,
        out_specs=[VMEM] * 2,
        scratch_shapes=list(scratch.values()),
        compiler_params=pltpu.CompilerParams(
            collective_id=0, has_side_effects=True, vmem_limit_bytes=60 * 2**20
        ),
        name="whole",
    )(
        queries,
        fresh_key_value,
        cache_key_value,
        out_proj,
        w_gate_up,
        w_down,
        residual,
        norm_gain.reshape(1, -1),
        route_ids.T,
        route_weights.T,
        placement.reshape(1, -1),
    )
    return pl.pallas_call(
        keep_kernel,
        out_shape=[jax.ShapeDtypeStruct((rows, width), narrow)] * 2,
        in_specs=[VMEM] * 2,
        out_specs=[VMEM] * 2,
        name="keep",
    )(hidden, result)


def solution(mesh):
    in_specs = (
        P(("groups", "ctx"), None),
        P(None, ("groups", "ctx"), None),
        P(None, ("groups", "ctx"), None),
        P(("groups", "ctx"), None),
        P(),
        P("ctx", None),
        P("ctx", None, None),
        P("ctx", None, None),
        P(("groups", "ctx"), None),
        P(("groups", "ctx"), None),
        P(),
    )
    out_specs = (P(("groups", "ctx"), None), P(("groups", "ctx"), None))
    return jax.shard_map(
        functools.partial(local, mesh.shape["ctx"]),
        mesh=mesh,
        in_specs=in_specs,
        out_specs=out_specs,
        check_vma=False,
    )
```

```python
import functools
import types
from collections import deque

import jax
import jax.numpy as jnp
from jax import lax
from jax.experimental import pallas as pl
from jax.experimental.pallas import tpu as pltpu
from jax.sharding import PartitionSpec as P

QUERY_HEADS = 32
KEY_VALUE_HEADS = 4
HEAD_SIZE = 128
TOPK = 8
COLUMNS_STEP = 1024
FF_STEP = 256
LANES = 128

epsilon = 1e-06

VMEM = pl.BlockSpec(memory_space=pltpu.VMEM)
ANY = pl.BlockSpec(memory_space=pl.ANY)
RIGHT, LEFT = 0, 1
PAIRS = ((RIGHT, 0), (LEFT, 1), (RIGHT, 1), (LEFT, 0))


def chip_at(q, m):
    return jnp.where(q < m // 2, 2 * q, 2 * (m - 1 - q) + 1)


def place_of(chip, m):
    return jnp.where(chip % 2 == 0, chip // 2, m - 1 - chip // 2)


def flip(value, key, size):
    total, bit = 0, 1
    while bit < size:
        total = total + (value // bit + key // bit) % 2 * bit
        bit *= 2
    return total


def greet(others):
    barrier = pltpu.get_barrier_semaphore()
    for other in others:
        pl.semaphore_signal(
            barrier, inc=1, device_id={"ctx": other}, device_id_type=pl.DeviceIdType.MESH
        )
    pl.semaphore_wait(barrier, len(others))


def remote(src, dst, send, recv, other):
    return pltpu.make_async_remote_copy(
        src_ref=src,
        dst_ref=dst,
        send_sem=send,
        recv_sem=recv,
        device_id={"ctx": other},
        device_id_type=pl.DeviceIdType.MESH,
    )


def landed(piece, sem):
    pltpu.make_async_copy(piece, piece, sem).wait()


def travels(way, half, d, reach):
    return d < reach or (d == reach and half == way)


def block_places(rows, experts):
    most = max(2, 3 * rows * TOPK // (2 * experts))
    return -(-most // 16) * 16


def whole_kernel(
    n,
    names,
    queries,
    fresh,
    cache,
    proj,
    gate_up,
    down,
    residual,
    gain,
    ids,
    route,
    placement,
    hidden,
    result,
    *scratch,
):
    s = types.SimpleNamespace(**dict(zip(names, scratch)))
    m, planes, reach = n // 2, n // 4, n // 4
    rows, width = residual.shape
    half_width = width // 2
    cols = [pl.ds(h * half_width, half_width) for h in range(2)]
    local_count, _, wide = gate_up.shape
    ff = wide // 2
    experts = placement.shape[1]
    places = s.rows_in.shape[2]
    per = QUERY_HEADS // n
    head_width = per * HEAD_SIZE
    share = n // KEY_VALUE_HEADS

    me = lax.axis_index("ctx")
    core, chip = me % 2, me // 2
    y, z = chip % 2, chip // 2

    def device(zz, yy, cc):
        return (zz * 2 + yy) * 2 + cc

    mate = device(z, y, 1 - core)
    across = device(z, 1 - y, core)
    started = []

    def send(src, dst, send_sem, recv_sem, other):
        copy = remote(src, dst, send_sem, recv_sem, other)
        copy.start()
        started.append(copy)

    def finish_sends():
        while started:
            started.pop(0).wait_send()

    greet([(me + j) % n for j in range(1, n)])

    mine, rank = me // share, me % share
    sources = ((cache, s.kv), (fresh, s.own))

    def lanes_of(head):
        return pl.ds(pl.multiple_of(head * HEAD_SIZE, HEAD_SIZE), HEAD_SIZE)

    local = []
    for kind, (src, dst) in enumerate(sources):
        copy = pltpu.make_async_copy(
            src.at[:, :, lanes_of(mine)], dst.at[:, mine, rank], s.kv_recv.at[kind, 0]
        )
        copy.start()
        local.append(copy)

    def spread_kv(kind):
        src, dst = sources[kind]
        for i in range(1, KEY_VALUE_HEADS):
            head = (mine + i) % KEY_VALUE_HEADS
            send(
                src.at[:, :, lanes_of(head)],
                dst.at[:, mine, rank],
                s.kv_send.at[kind, i],
                s.kv_recv.at[kind, i],
                head * share + rank,
            )

    spread_kv(0)
    spread_kv(1)

    copy = pltpu.make_async_copy(
        queries.at[:, pl.ds(pl.multiple_of(me * head_width, LANES), head_width)],
        s.q.at[me],
        s.q_recv.at[me],
    )
    copy.start()

    def send_queries(key, start=True):
        for dy in (1, 0):
            for dc in (0, 1):
                if (key, dy, dc) == (0, 0, 0):
                    continue
                other = device(flip(z, key, planes), (y + dy) % 2, (core + dc) % 2)
                copy = remote(
                    queries.at[:, pl.ds(pl.multiple_of(other * head_width, LANES), head_width)],
                    s.q.at[me],
                    s.q_send.at[key * 4 + dy * 2 + dc],
                    s.q_recv.at[me],
                    other,
                )
                if start:
                    copy.start()
                else:
                    copy.wait_send()

    for key in range(planes // 2 - 1, -1, -1):
        send_queries(key)
    send(proj, s.proj_mate, s.mate_send.at[m], s.mate_recv.at[m], mate)
    weights = [
        pltpu.make_async_copy(proj, s.proj_mine, s.load.at[0]),
        pltpu.make_async_copy(gate_up, s.gate_up, s.load.at[1]),
        pltpu.make_async_copy(down, s.down, s.load.at[2]),
    ]
    for copy in weights:
        copy.start()

    def table_copy(j):
        other = (me + j) % n
        return remote(
            s.table.at[other // 2], s.tables.at[me], s.t_send.at[j], s.t_recv.at[j], other
        )

    def fill_tables():
        scores = route[...]
        scores = scores / jnp.sum(scores, axis=0, keepdims=True)
        listed = lax.broadcasted_iota(jnp.int32, (experts, rows), 0)
        by_expert = jnp.zeros((experts, rows), jnp.float32)
        for k in range(TOPK):
            by_expert = by_expert + jnp.where(listed == ids[k : k + 1], scores[k : k + 1], 0.0)
        by_expert = jnp.concatenate(
            [by_expert, jnp.zeros((experts, LANES - rows), jnp.float32)], axis=1
        ).astype(jnp.bfloat16)
        moved = jnp.where(
            lax.broadcasted_iota(jnp.int32, (experts, experts), 0) == placement[...], 1.0, 0.0
        ).astype(jnp.bfloat16)
        by_slot = jnp.dot(moved, by_expert, preferred_element_type=jnp.float32)
        named = jnp.where(by_slot > 0, 1.0, 0.0)
        before = jnp.where(
            lax.broadcasted_iota(jnp.int32, (LANES, LANES), 0)
            < lax.broadcasted_iota(jnp.int32, (LANES, LANES), 1),
            1.0,
            0.0,
        ).astype(jnp.bfloat16)
        ranks = jnp.dot(named.astype(jnp.bfloat16), before, preferred_element_type=jnp.float32)
        ranks = jnp.where(by_slot > 0, ranks, -1.0)
        pair = 2 * local_count
        for c in range(m):
            s.table[c, 0:pair, :] = ranks[c * pair : (c + 1) * pair]
            s.table[c, pair : 2 * pair, :] = by_slot[c * pair : (c + 1) * pair]
        s.tables[me] = s.table[chip]
        for j in range(1, n):
            table_copy(j).start()

    steps = []
    bit = 2
    while bit < share:
        steps.append(bit)
        bit *= 2
    final = len(steps)
    groups = tuple(range(KEY_VALUE_HEADS))
    outer = jnp.logical_or(z < planes // 4, z >= planes - planes // 4)

    def send_far():
        for key in range(planes - 1, planes // 2 - 1, -1):
            send_queries(key)

    def slot(kind, i, k):
        g = (mine + KEY_VALUE_HEADS - i) % KEY_VALUE_HEADS
        return sources[kind][1].at[:, g, flip(rank, k, share)]

    def passing(kind, i, number, k):
        step = 1 if number == final else steps[number]
        return remote(
            slot(kind, i, k),
            slot(kind, i, k),
            s.fw_send.at[kind, i, number, k // 2],
            s.fw_recv.at[kind, i, k + step],
            mate if number == final else mine * share + flip(rank, step, share),
        )

    def pass_on(kind, chosen):
        known = [0]
        for number, step in enumerate(steps):
            for i in chosen:
                if number == 0:
                    if i > 0:
                        landed(slot(kind, i, 0), s.kv_recv.at[kind, i])
                    else:
                        local[kind].wait()
                for k in known:
                    passing(kind, i, number, k).start()
                if number == 0:
                    passing(kind, i, final, 0).start()
            for i in chosen:
                for k in known:
                    landed(slot(kind, i, k + step), s.fw_recv.at[kind, i, k + step])
                    passing(kind, i, final, k + step).start()
            known = known + [k + step for k in known]

    def pass_end(kind, chosen):
        for i in chosen:
            for k in range(0, share, 2):
                landed(slot(kind, i, k + 1), s.fw_recv.at[kind, i, k + 1])

    pass_on(0, groups)
    send_far()
    pass_on(1, groups)
    pass_end(0, groups)
    pass_end(1, groups)
    landed(s.proj_mate, s.mate_recv.at[m])
    weights[0].wait()

    key_count = s.kv.shape[3]
    scale = HEAD_SIZE ** (-0.5)

    near = flip(z, 1, planes)

    def target(t):
        turn, above, lower = t - 1, planes - 1 - z, z < planes // 2
        skipped = jnp.where(
            lower,
            jnp.where(z % 2 == 0, above - 1, planes - 2),
            jnp.where(z % 2 == 1, z - 1, planes - 2),
        )
        turn = turn + jnp.where(turn >= skipped, 1, 0)
        rising = jnp.where(turn < above, planes - 1 - turn, turn - above)
        falling = jnp.where(turn < z, turn, planes - 1 - (turn - z))
        beyond = jnp.where(lower, rising, falling)
        return jnp.where(t == 0, near, jnp.where(t == planes - 1, z, beyond))

    def attend(t):
        @pl.loop(0, 2)
        def _(line):
            c = target(t) * 2 + (y + 1 + line) % 2
            for cc in range(2):
                landed(s.q.at[2 * c + cc], s.q_recv.at[2 * c + cc])
            keys = s.kv[0].reshape(n * key_count, HEAD_SIZE)
            values = s.kv[1].reshape(n * key_count, HEAD_SIZE)
            fresh_key = s.own[0, (2 * c) // share, pl.ds((2 * c) % share, 2)]
            fresh_key = fresh_key.reshape(2 * rows, HEAD_SIZE).astype(jnp.float32)
            fresh_value = s.own[1, (2 * c) // share, pl.ds((2 * c) % share, 2)]
            fresh_value = fresh_value.reshape(2 * rows, HEAD_SIZE).astype(jnp.float32)
            for h in range(per):
                lanes = slice(h * HEAD_SIZE, (h + 1) * HEAD_SIZE)
                q = s.q[pl.ds(2 * c, 2), :, lanes].reshape(2 * rows, HEAD_SIZE)
                scores = lax.dot_general(
                    q, keys, (((1,), (1,)), ((), ())), preferred_element_type=jnp.float32
                )
                own = jnp.sum(q.astype(jnp.float32) * fresh_key, axis=-1, keepdims=True)
                peak = jnp.maximum(own, jnp.max(scores, axis=-1, keepdims=True))
                weight = jnp.exp((scores - peak) * scale)
                own = jnp.exp((own - peak) * scale)
                total = jnp.sum(weight, axis=-1, keepdims=True) + own
                mixed = jnp.dot(
                    weight.astype(jnp.bfloat16), values, preferred_element_type=jnp.float32
                )
                mixed = (mixed + own * fresh_value) / total
                s.att[c, :, :, lanes] = mixed.astype(jnp.bfloat16).reshape(2, rows, HEAD_SIZE)
            remote(
                s.att.at[c, 1 - core],
                s.att_mate.at[c],
                s.mate_send.at[c],
                s.mate_recv.at[c],
                mate,
            ).start()

    def project(t):
        zd = target(t)
        chips = [zd * 2 + (1 - y), zd * 2 + y]
        for c in chips:
            landed(s.att_mate.at[c], s.mate_recv.at[c])
        left = jnp.concatenate([s.att[c, core] for c in chips], axis=0)
        left_mate = jnp.concatenate([s.att_mate[c] for c in chips], axis=0)
        for half in range(2):

            for i in range(half_width // COLUMNS_STEP):
                part = pl.ds(i * COLUMNS_STEP, COLUMNS_STEP)
                at = pl.ds(half * half_width + i * COLUMNS_STEP, COLUMNS_STEP)
                product = jnp.dot(
                    left, s.proj_mine[:, at], preferred_element_type=jnp.float32
                ) + jnp.dot(left_mate, s.proj_mate[:, at], preferred_element_type=jnp.float32)
                if half == 0:
                    s.outgoing[0, zd, half, :, part] = product[:rows].astype(jnp.bfloat16)
                else:

                    @pl.when(t < planes - 1)
                    def _():
                        s.outgoing[0, zd, half, :, part] = product[:rows].astype(jnp.bfloat16)

                    @pl.when(t == planes - 1)
                    def _():
                        if i == 0:
                            landed(s.turned, s.turn_recv.at[0])
                        total = product[:rows] + s.turned[:, part].astype(jnp.float32)
                        s.outgoing[0, zd, half, :, part] = total.astype(jnp.bfloat16)

                s.outgoing[1, zd, half, :, part] = product[rows:].astype(jnp.bfloat16)

            def go_across(half=half):
                remote(
                    s.outgoing.at[0, zd, half],
                    s.y_in.at[zd, half],
                    s.y_send.at[zd, half],
                    s.y_recv.at[zd, half],
                    across,
                ).start()

            if half == 0:
                go_across()
            else:
                pl.when(t > 0)(go_across)

                @pl.when(t == 0)
                def _():
                    remote(
                        s.outgoing.at[0, zd, half],
                        s.turned,
                        s.y_send.at[zd, half],
                        s.turn_recv.at[0],
                        device(near, y, core),
                    ).start()


    def from_line(zd, way, half):
        landed(s.incoming.at[way, zd, half], s.z_recv.at[way, zd, half])

    def relay(t):
        zd = target(t)
        way = jnp.where(zd > z, RIGHT, LEFT)
        inner = jnp.where(zd > z, z > 0, z < planes - 1)
        other = device(jnp.where(zd > z, z + 1, z - 1), y, core)
        for half in range(2):
            s.part[half] = s.outgoing[1, zd, half].astype(jnp.float32)

            def from_across(half=half):
                landed(s.y_in.at[zd, half], s.y_recv.at[zd, half])
                s.part[half] = s.part[half] + s.y_in[zd, half].astype(jnp.float32)

            if half == 0:
                from_across()
            else:
                pl.when(t > 0)(from_across)

            @pl.when(inner)
            def _():
                from_line(zd, way, half)
                s.part[half] = s.part[half] + s.incoming[way, zd, half].astype(jnp.float32)

            s.outgoing[1, zd, half] = s.part[half].astype(jnp.bfloat16)
            remote(
                s.outgoing.at[1, zd, half],
                s.incoming.at[way, zd, half],
                s.z_send.at[zd, half],
                s.z_recv.at[way, zd, half],
                other,
            ).start()


    @pl.loop(0, planes + 2)
    def _(u):
        @pl.when(u == 1)
        def _():
            fill_tables()

        @pl.when(u < planes)
        def _():
            attend(u)

        @pl.when(u < planes)
        def _():
            project(u)

        early = jnp.logical_and(outer, jnp.logical_and(u > 1, u <= planes))

        @pl.when(early)
        def _():
            relay((u - 1) % (planes - 1))

        @pl.when(jnp.logical_and(jnp.logical_not(outer), u > 2))
        def _():
            relay((u - 2) % (planes - 1))

    squares = 0.0
    for half in range(2):
        landed(s.y_in.at[z, half], s.y_recv.at[z, half])
        s.part[half] = (
            s.outgoing[1, z, half].astype(jnp.float32)
            + s.y_in[z, half].astype(jnp.float32)
            + residual[:, cols[half]].astype(jnp.float32)
        )
        for way, there in ((RIGHT, z > 0), (LEFT, z < planes - 1)):

            @pl.when(there)
            def _():
                from_line(z, way, half)
                s.part[half] = s.part[half] + s.incoming[way, z, half].astype(jnp.float32)

        value = s.part[half].astype(jnp.bfloat16)
        hidden[:, cols[half]] = value
        value = value.astype(jnp.float32)
        squares = squares + jnp.sum(value * value, axis=-1, keepdims=True)
    factor = lax.rsqrt(squares / width + epsilon)
    for half in range(2):
        value = hidden[:, cols[half]].astype(jnp.float32)
        s.normed[:, cols[half]] = (value * factor * gain[:, cols[half]]).astype(jnp.bfloat16)

    p = place_of(chip, m)

    def at(offset, c):
        return chip_at((p + offset + m) % m, m) * 2 + c

    neighbour = (at(1, core), at(-1, core))
    offsets = [0]
    for d in range(1, reach):
        offsets += [-d, d]
    offsets.append(reach)

    def forward(src, owner, way, half, d):
        send(
            src,
            s.held.at[owner, :, cols[half]],
            s.ring_send.at[way, d, half],
            s.ring_recv.at[way, d, half],
            neighbour[way],
        )

    for way, half in PAIRS:
        forward(s.normed.at[:, cols[half]], me, way, half, 0)
    send(s.normed, s.held.at[me], s.pass_send.at[0, 0, 0], s.pass_recv.at[0, 0, 0], mate)
    s.held[me] = s.normed[...]
    for key in range(planes):
        zd = flip(z, key, planes)
        for half in range(2):
            remote(
                s.outgoing.at[0, zd, half],
                s.y_in.at[zd, half],
                s.y_send.at[zd, half],
                s.y_recv.at[zd, half],
                across,
            ).wait_send()
            if key > 0:
                remote(
                    s.outgoing.at[1, zd, half],
                    s.incoming.at[0, zd, half],
                    s.z_send.at[zd, half],
                    s.z_recv.at[0, zd, half],
                    across,
                ).wait_send()
    for c in range(m):
        remote(
            s.att.at[c, 1 - core], s.att_mate.at[c], s.mate_send.at[c], s.mate_recv.at[c], mate
        ).wait_send()
    for key in range(planes):
        send_queries(key, start=False)
    for kind in range(2):
        for i in groups:
            known = [0]
            for number, step in enumerate(steps):
                for k in known:
                    passing(kind, i, number, k).wait_send()
                known = known + [k + step for k in known]
            for k in known:
                passing(kind, i, final, k).wait_send()
    for j in range(1, n):
        table_copy(j).wait_send()
        landed(s.tables.at[(me + n - j) % n], s.t_recv.at[j])

    def wait_mate(offset):
        if offset == 0:
            landed(s.held.at[mate], s.pass_recv.at[0, 0, 0])
            return
        d = abs(offset)
        for way, half in PAIRS:
            if travels(way, half, d, reach) and (d == reach or (way == RIGHT) == (offset < 0)):
                landed(
                    s.held.at[at(offset, 1 - core), :, cols[half]], s.pass_recv.at[way, d, half]
                )

    spots = lax.broadcasted_iota(jnp.int32, (places, LANES), 0).astype(jnp.float32)

    def pick(offset):
        k = offsets.index(offset)
        wait_mate(offset)
        for cc in range(2):
            owner = at(offset, cc)
            marks = []
            for e in range(local_count):
                place = s.tables[owner, pl.ds(core * local_count + e, 1), :]
                marks.append(jnp.where(spots == place, 1.0, 0.0))
            marks = jnp.concatenate(marks, axis=0)[:, :rows].astype(jnp.bfloat16)

            for i in range(width // COLUMNS_STEP):
                part = pl.ds(i * COLUMNS_STEP, COLUMNS_STEP)
                picked = jnp.dot(
                    marks, s.held[owner, :, part], preferred_element_type=jnp.float32
                ).astype(jnp.bfloat16)
                for e in range(local_count):
                    s.rows_in[2 * k + cc, e, :, part] = picked[e * places : (e + 1) * places]

        owner = at(offset, core)
        shares = []
        for side in (core, 1 - core):
            for e in range(local_count):
                place = s.tables[owner, pl.ds(side * local_count + e, 1), :]
                portion = s.tables[owner, pl.ds((2 + side) * local_count + e, 1), :]
                shares.append(jnp.where(spots == place, portion, 0.0))
        shares = jnp.concatenate(shares, axis=0).T
        s.mix[k] = shares[:rows].astype(jnp.bfloat16)

    def expand(e, f, first, last):
        count = (last - first) * places
        x = s.rows_in[first:last, e].reshape(count, width)
        gate = jnp.dot(
            x, s.gate_up[e, :, f * FF_STEP : (f + 1) * FF_STEP], preferred_element_type=jnp.float32
        )
        up = jnp.dot(
            x,
            s.gate_up[e, :, ff + f * FF_STEP : ff + (f + 1) * FF_STEP],
            preferred_element_type=jnp.float32,
        )
        value = gate / (1.0 + jnp.exp(-gate)) * up
        s.active[e, first * places : last * places, f * FF_STEP : (f + 1) * FF_STEP] = value.astype(
            jnp.bfloat16
        )

    def contract(e, first, last):
        count = (last - first) * places

        for i in range(width // COLUMNS_STEP):
            part = pl.ds(i * COLUMNS_STEP, COLUMNS_STEP)
            value = jnp.dot(
                s.active[e, first * places : last * places, :],
                s.down[e, :, part],
                preferred_element_type=jnp.float32,
            )
            s.rows_in[first:last, e, :, part] = value.astype(jnp.bfloat16).reshape(
                last - first, places, COLUMNS_STEP
            )

    def trade(first, last):
        for k in reversed(range(first // 2, last // 2)):
            send(
                s.rows_in.at[2 * k + 1 - core],
                s.rows_mate.at[k],
                s.trade_send.at[k],
                s.trade_recv.at[k],
                mate,
            )

    def expert_jobs(first, last):
        jobs = []
        for e in range(local_count):
            for f in range(ff // FF_STEP):
                jobs.append(functools.partial(expand, e, f, first, last))
        for e in range(local_count):
            jobs.append(functools.partial(contract, e, first, last))
        jobs.append(functools.partial(trade, first, last))
        return jobs

    early, later = 2 * (2 * reach - 5), 2 * (2 * reach - 3)
    jobs = deque()
    waits = {d: sum(travels(way, half, d, reach) for way, half in PAIRS) for d in range(1, reach + 1)}
    left = sum(waits.values())

    def level(d):
        found = [o for o in offsets if abs(o) == d]
        return [functools.partial(pick, o) for o in found]

    for d in range(1, reach + 1):
        jobs.extend(level(d - 1))
        if d == reach - 2:
            for copy in weights[1:]:
                jobs.append(copy.wait)
            jobs.extend(expert_jobs(0, early))
        if d == reach - 1:
            jobs.extend(expert_jobs(early, later))
        for way, half in PAIRS:
            if not travels(way, half, d, reach):
                continue
            owner = at(-d if way == RIGHT else d, core)
            piece = s.held.at[owner, :, cols[half]]
            landed(piece, s.ring_recv.at[way, d - 1, half])
            if travels(way, half, d + 1, reach):
                forward(piece, owner, way, half, d)
            send(piece, piece, s.pass_send.at[way, d, half], s.pass_recv.at[way, d, half], mate)
            for _ in range(min(2, len(jobs))):
                jobs.popleft()()
            left -= 1
    jobs.extend(level(reach))
    while jobs:
        jobs.popleft()()
    for job in expert_jobs(later, 2 * m):
        job()

    traded = set()

    def portion(offset, half, i):
        k = offsets.index(offset)
        part = pl.ds(half * half_width + i * COLUMNS_STEP, COLUMNS_STEP)
        depth = local_count * places
        both = jnp.concatenate(
            [
                s.rows_in[2 * k + core, :, :, part].reshape(depth, COLUMNS_STEP),
                s.rows_mate[k, :, :, part].reshape(depth, COLUMNS_STEP),
            ],
            axis=0,
        )
        return jnp.dot(s.mix[k], both, preferred_element_type=jnp.float32)

    def meet(offset):
        k = offsets.index(offset)
        if k not in traded:
            landed(s.rows_mate.at[k], s.trade_recv.at[k])
            traded.add(k)

    for d in range(reach, 0, -1):
        for way, half in ((RIGHT, 1), (LEFT, 0), (RIGHT, 0), (LEFT, 1)):
            if not travels(way, half, d, reach):
                continue
            offset = d if (way == RIGHT or d == reach) else -d
            meet(offset)
            adds = travels(way, half, d + 1, reach)
            if adds:
                landed(s.incoming.at[way, d, half], s.back_recv.at[way, d, half])

            for i in range(half_width // COLUMNS_STEP):
                part = pl.ds(i * COLUMNS_STEP, COLUMNS_STEP)
                total = portion(offset, half, i)
                if adds:
                    total = total + s.incoming[way, d, half, :, part].astype(jnp.float32)
                s.outgoing[way, d - 1, half, :, part] = total.astype(jnp.bfloat16)

            send(
                s.outgoing.at[way, d - 1, half],
                s.incoming.at[way, d - 1, half],
                s.back_send.at[way, d - 1, half],
                s.back_recv.at[way, d - 1, half],
                neighbour[way],
            )
    meet(0)
    for half in range(2):
        for way in (RIGHT, LEFT):
            landed(s.incoming.at[way, 0, half], s.back_recv.at[way, 0, half])

        for i in range(half_width // COLUMNS_STEP):
            part = pl.ds(i * COLUMNS_STEP, COLUMNS_STEP)
            out = pl.ds(half * half_width + i * COLUMNS_STEP, COLUMNS_STEP)
            total = portion(0, half, i)
            for way in (RIGHT, LEFT):
                total = total + s.incoming[way, 0, half, :, part].astype(jnp.float32)
            result[:, out] = total.astype(jnp.bfloat16)

    finish_sends()


def keep_kernel(hidden, result, hidden_out, result_out):
    hidden_out[...] = hidden[...]
    result_out[...] = result[...]


def local(
    n,
    queries,
    fresh_key_value,
    cache_key_value,
    residual,
    norm_gain,
    out_proj,
    w_gate_up,
    w_down,
    route_ids,
    route_weights,
    placement,
):
    rows, width = residual.shape
    experts = placement.shape[0]
    local_count, _, wide = w_gate_up.shape
    key_count = cache_key_value.shape[1]
    places = block_places(rows, experts)
    m, planes, reach = n // 2, n // 4, n // 4
    share = n // KEY_VALUE_HEADS
    head_width = QUERY_HEADS // n * HEAD_SIZE
    levels = max(1, share.bit_length() - 2)
    half = width // 2
    narrow = jnp.bfloat16
    sems = pltpu.SemaphoreType.DMA
    scratch = dict(
        kv=pltpu.VMEM((2, KEY_VALUE_HEADS, share, key_count, HEAD_SIZE), narrow),
        own=pltpu.VMEM((2, KEY_VALUE_HEADS, share, rows, HEAD_SIZE), narrow),
        q=pltpu.VMEM((n, rows, head_width), narrow),
        proj_mine=pltpu.VMEM((head_width, width), narrow),
        proj_mate=pltpu.VMEM((head_width, width), narrow),
        gate_up=pltpu.VMEM(w_gate_up.shape, narrow),
        down=pltpu.VMEM(w_down.shape, narrow),
        table=pltpu.VMEM((m, 4 * local_count, LANES), jnp.float32),
        tables=pltpu.VMEM((n, 4 * local_count, LANES), jnp.float32),
        att=pltpu.VMEM((m, 2, rows, head_width), narrow),
        att_mate=pltpu.VMEM((m, rows, head_width), narrow),
        part=pltpu.VMEM((2, rows, half), jnp.float32),
        turned=pltpu.VMEM((rows, half), narrow),
        y_in=pltpu.VMEM((planes, 2, rows, half), narrow),
        outgoing=pltpu.VMEM((2, reach, 2, rows, half), narrow),
        incoming=pltpu.VMEM((2, reach, 2, rows, half), narrow),
        normed=pltpu.VMEM((rows, width), narrow),
        held=pltpu.VMEM((n, rows, width), narrow),
        rows_in=pltpu.VMEM((n, local_count, places, width), narrow),
        rows_mate=pltpu.VMEM((m, local_count, places, width), narrow),
        active=pltpu.VMEM((local_count, n * places, wide // 2), narrow),
        mix=pltpu.VMEM((m, rows, 2 * local_count * places), narrow),
        kv_send=sems((2, KEY_VALUE_HEADS)),
        kv_recv=sems((2, KEY_VALUE_HEADS)),
        fw_send=sems((2, KEY_VALUE_HEADS, levels + 1, share // 2)),
        fw_recv=sems((2, KEY_VALUE_HEADS, share)),
        q_send=sems((n,)),
        q_recv=sems((n,)),
        t_send=sems((n,)),
        t_recv=sems((n,)),
        load=sems((3,)),
        mate_send=sems((m + 1,)),
        mate_recv=sems((m + 1,)),
        y_send=sems((planes, 2)),
        y_recv=sems((planes, 2)),
        turn_recv=sems((1,)),
        z_send=sems((planes, 2)),
        z_recv=sems((2, planes, 2)),
        ring_send=sems((2, reach, 2)),
        ring_recv=sems((2, reach, 2)),
        pass_send=sems((2, reach + 1, 2)),
        pass_recv=sems((2, reach + 1, 2)),
        trade_send=sems((m,)),
        trade_recv=sems((m,)),
        back_send=sems((2, reach, 2)),
        back_recv=sems((2, reach, 2)),
    )
    hidden, result = pl.pallas_call(
        functools.partial(whole_kernel, n, tuple(scratch)),
        out_shape=[jax.ShapeDtypeStruct((rows, width), narrow)] * 2,
        in_specs=[ANY] * 6 + [VMEM] * 5,
        out_specs=[VMEM] * 2,
        scratch_shapes=list(scratch.values()),
        compiler_params=pltpu.CompilerParams(
            collective_id=0, has_side_effects=True, vmem_limit_bytes=60 * 2**20
        ),
        name="whole",
    )(
        queries,
        fresh_key_value,
        cache_key_value,
        out_proj,
        w_gate_up,
        w_down,
        residual,
        norm_gain.reshape(1, -1),
        route_ids.T,
        route_weights.T,
        placement.reshape(1, -1),
    )
    return pl.pallas_call(
        keep_kernel,
        out_shape=[jax.ShapeDtypeStruct((rows, width), narrow)] * 2,
        in_specs=[VMEM] * 2,
        out_specs=[VMEM] * 2,
        name="keep",
    )(hidden, result)


def solution(mesh):
    in_specs = (
        P(("groups", "ctx"), None),
        P(None, ("groups", "ctx"), None),
        P(None, ("groups", "ctx"), None),
        P(("groups", "ctx"), None),
        P(),
        P("ctx", None),
        P("ctx", None, None),
        P("ctx", None, None),
        P(("groups", "ctx"), None),
        P(("groups", "ctx"), None),
        P(),
    )
    out_specs = (P(("groups", "ctx"), None), P(("groups", "ctx"), None))
    return jax.shard_map(
        functools.partial(local, mesh.shape["ctx"]),
        mesh=mesh,
        in_specs=in_specs,
        out_specs=out_specs,
        check_vma=False,
    )
```
